32 devices in a mesh: scen: 2 (over y), dw: 4 (over x, core), reg: 4 (over z).
Axes of the slice: x: 2, y: 2, z: 4, core: 2. Of those that a mesh axis runs over, the one named last changes fastest.
Arguments:
- load_base: float32 [96, 65536], P(None, ('scen', 'dw', 'reg')), parts along dimension 1, may hold values from -24 to 24
- kkt_inverse: float32 [64, 96, 96], replicated, may hold values from -1 to 2
- archetype: int32 [65536], P(('scen', 'dw', 'reg')), parts along dimension 0, may hold values from 0 to 63
- feeder: int32 [65536], P(('scen', 'dw', 'reg')), parts along dimension 0, may hold values from 0 to 255, as said below
- live_counts: int32 [32, 4], P(('scen', 'dw', 'reg')), parts along dimension 0, may hold values from 1 to 512, as said below
- feeder_cap: int32 [512], P(('scen', 'dw', 'reg')), parts along dimension 0, may hold values from 1000 to 11999
- dual_start: float32 [512, 96], P(('scen', 'dw', 'reg')), parts along dimension 0, may hold values from 0 to 1
- balance_target: float32 [192], P('scen'), parts along dimension 0, may hold values from -6 to 6
Outputs:
- roster: float32 [96, 65536], P(None, ('scen', 'dw', 'reg')), parts along dimension 1
- feeder_duals: float32 [512, 96], P(('scen', 'dw', 'reg')), parts along dimension 0
- balance_dual: float32 [192], P('scen'), parts along dimension 0
The draws below stay inside these ranges and needn't reach their ends.
There are 2 independent parts, one for each index of `scen`. The reference program is written for one: setup_inputs(seed, part) draws one part's arguments, and reference() takes and returns one part's arrays. A program takes and returns all parts, laid end to end along the dimension named above; an argument that names none is the same for every part. Nothing has to cross between parts.
Inputs may be any that keep to these rules, and one draw needn't show every extreme that they name: The feeder of the dwelling in slot s of the device at index j along dw and r along reg lies in block k * 4 + r of 16 feeders, where k = s // 512. `live_counts`: row d (devices in the order dw+reg) gives for each block k the number of leading slots of that block that hold a dwelling; the other slots are empty. Every row has a block of 512.
All inputs are finite; a program needn't handle non-finite values.
Results may differ from the reference program's by a relative error of at most 0.0003.
Values sent between devices are 32-bit elements; how exact they have to be, the bound alone decides.
No kernel may reach another device: no remote copies, remote signals or barrier semaphores. Data moves between devices by JAX's collectives and lax.ppermute only.
A program may use at most 64 MiB of HBM per device.

```python
import math
import jax
import jax.numpy as jnp
from jax import lax

T_STEPS = 96
ARCH = 64
DW_DEV = 2048
FD_DEV = 16
ITERS = 2
SEG = 512
DWELLINGS = 32768
FEEDERS = 256
N_DW = 4
N_REG = 4


def draw_load_base(key, part):
    first_key = jax.random.fold_in(key, 0)
    row_index = jnp.arange(DWELLINGS, dtype=jnp.float32)
    row_scale = 1.0 + 2.0 * row_index / DWELLINGS
    rough = jnp.clip(jax.random.normal(first_key, (T_STEPS, DWELLINGS), jnp.float32), -6.0, 6.0)
    values = row_scale[None, :] * rough
    return jnp.clip(values, -24.0, 24.0)


def draw_kkt_inverse(key, part):
    first_key, second_key = jax.random.split(key)
    identity = (jnp.arange(T_STEPS)[:, None] == jnp.arange(T_STEPS)[None, :]).astype(jnp.float32)
    spread = 0.4 / math.sqrt(T_STEPS)
    diagonal = jax.random.uniform(first_key, (ARCH, T_STEPS, 1), jnp.float32, 0.5, 1.5)
    others = jnp.clip(jax.random.normal(second_key, (ARCH, T_STEPS, T_STEPS), jnp.float32), -4.0, 4.0) * spread
    return identity[None] * diagonal + (1.0 - identity[None]) * others


def draw_feeder(key, part):
    first_key = jax.random.fold_in(key, 11)
    second_key = jax.random.fold_in(key, 12)
    third_key = jax.random.fold_in(key, 13)
    row_index = jnp.arange(DWELLINGS, dtype=jnp.int32)
    device_index = row_index // DW_DEV
    region_index = device_index % N_REG
    block_index = row_index % DW_DEV // SEG
    owner_block = block_index * N_REG + region_index
    first_pick = jax.random.randint(first_key, (DWELLINGS,), 0, FD_DEV, jnp.int32)
    second_pick = jax.random.randint(second_key, (DWELLINGS,), 0, FD_DEV, jnp.int32)
    offsets = jax.random.randint(third_key, (DWELLINGS // SEG,), 0, FD_DEV, jnp.int32)
    local_label = (jnp.minimum(first_pick, second_pick) + offsets[row_index // SEG]) % FD_DEV
    return (owner_block * FD_DEV + local_label).astype(jnp.int32)


def draw_live_counts(key, part):
    first_key = jax.random.fold_in(key, 21)
    second_key = jax.random.fold_in(key, 22)
    row_total = N_DW * N_REG
    lowest = max(1, SEG // 4)
    counts_drawn = jax.random.randint(first_key, (row_total, N_DW), lowest, SEG + 1, jnp.int32)
    full_block = jax.random.randint(second_key, (row_total, 1), 0, N_DW, jnp.int32)
    block_index = jnp.arange(N_DW, dtype=jnp.int32)[None, :]
    return jnp.where(block_index == full_block, SEG, counts_drawn).astype(jnp.int32)


def touch_ends(values, key, least, high):
    longest = values.shape.index(max(values.shape))
    spots = []
    for shift in (0, 1):
        where = [jax.random.randint(jax.random.fold_in(key, axis), (), 0, length) for axis, length in enumerate(values.shape)]
        where[longest] = (where[longest] + shift) % values.shape[longest]
        spots.append(tuple(where))
    return values.at[spots[0]].set(least).at[spots[1]].set(high)


def level_of(stream_key, extent, cuts, smallest, top_value):
    level = 1.0
    for dim, shards_of in cuts:
        heights = jax.random.uniform(jax.random.fold_in(jax.random.fold_in(stream_key, 6), dim), (shards_of,), jnp.float32, smallest / len(cuts), top_value / len(cuts))
        level = level * jnp.repeat(jnp.exp(heights), extent[dim] // shards_of).reshape((-1,) + (1,) * (len(extent) - 1 - dim))
    return level


def scatter_about(rng, extent, width, limit, kind=jnp.bfloat16):
    array = jax.random.normal(rng, extent, jnp.float32) * width
    return jnp.minimum(jnp.maximum(array, -limit), limit).astype(kind)


def setup_inputs(seed: int = 0, part: int = 0) -> dict:
    splits = jax.random.split(jax.random.key(seed), 9)
    part_splits = jax.random.split(jax.random.fold_in(splits[8], part), 9)
    load_base = draw_load_base(jax.random.fold_in(jax.random.fold_in(splits[8], part), 71), part)
    kkt_inverse = draw_kkt_inverse(jax.random.fold_in(splits[8], 71), part)
    archetype = touch_ends(jax.random.randint(part_splits[2], (DWELLINGS,), 0, ARCH), jax.random.fold_in(part_splits[2], 1), 0, ARCH - 1).astype(jnp.int32)
    feeder = draw_feeder(jax.random.fold_in(jax.random.fold_in(splits[8], part), 71), part)
    live_counts = draw_live_counts(jax.random.fold_in(jax.random.fold_in(splits[8], part), 71), part)
    feeder_cap = touch_ends(jax.random.randint(part_splits[5], (FEEDERS,), 1000, 12000), jax.random.fold_in(part_splits[5], 1), 1000, 11999).astype(jnp.int32)
    dual_start = jnp.clip(1.0 * jax.random.uniform(part_splits[6], (FEEDERS, T_STEPS), jnp.float32) ** level_of(part_splits[6], (FEEDERS, T_STEPS), ((0, 16),), -0.2, 0.2), 0.0, 1.0)
    balance_target = scatter_about(part_splits[7], (T_STEPS,), 1.0, 6.0, jnp.float32)
    return {"load_base": load_base, "kkt_inverse": kkt_inverse, "archetype": archetype, "feeder": feeder, "live_counts": live_counts, "feeder_cap": feeder_cap, "dual_start": dual_start, "balance_target": balance_target}


rho_weight = 0.5
dual_rate = 0.1
balance_rate = 1.0

def apply_inverse(kkt_inverse, archetype, rhs_field, block_width):
    steps_count, rows_count = rhs_field.shape
    block_count = rows_count // block_width
    blocks_in = rhs_field.reshape(steps_count, block_count, block_width).transpose(1, 0, 2)
    labels_in = archetype.reshape(block_count, block_width)

    def one_block(operand):
        labels, columns_in = operand
        picked = jnp.take(kkt_inverse, labels, axis=0)
        return jnp.einsum('bts,sb->tb', picked, columns_in, precision=lax.Precision.HIGHEST)
    out_blocks = lax.map(one_block, (labels_in, blocks_in))
    return out_blocks.transpose(1, 0, 2).reshape(steps_count, rows_count)

def reference(load_base, kkt_inverse, archetype, feeder, live_counts, feeder_cap, dual_start, balance_target):
    slot_index = jnp.arange(SEG, dtype=jnp.int32)
    live_mask = (live_counts[:, :, None] > slot_index[None, None, :]).reshape(DWELLINGS).astype(jnp.float32)
    cap_value = feeder_cap.astype(jnp.float32) * 0.001
    inv_root = 1.0 / math.sqrt(DWELLINGS)
    block_width = math.gcd(DWELLINGS, 1024)
    feeder_duals = dual_start
    balance_dual = jnp.zeros((T_STEPS,), jnp.float32)
    roster = jnp.zeros((T_STEPS, DWELLINGS), jnp.float32)
    for sweep_index in range(ITERS):
        dwelling_duals = jnp.take(feeder_duals, feeder, axis=0).T
        rhs_field = load_base - dwelling_duals - balance_dual[:, None] + rho_weight * roster
        roster = apply_inverse(kkt_inverse, archetype, rhs_field, block_width) * live_mask[None, :]
        feeder_loads = jax.ops.segment_sum(roster.T, feeder, num_segments=FEEDERS)
        system_load = lax.optimization_barrier(jnp.sum(roster, axis=1))
        feeder_duals = jnp.maximum(feeder_duals + dual_rate * (feeder_loads - cap_value[:, None]), 0.0)
        balance_dual = balance_dual + balance_rate * (system_load * inv_root - balance_target)
    return (roster, feeder_duals, balance_dual)
```

```python
import math

import jax
import jax.numpy as jnp
from jax import lax
from jax.experimental import pallas as pl
from jax.experimental.pallas import tpu as pltpu
from jax.sharding import PartitionSpec as P

rho_weight = 0.5
dual_rate = 0.1
balance_rate = 1.0

LANES = 128
ROWS = 256
WIN = 64
EXTRA = 32
VMEM_BYTES = 56 * 1024 * 1024

F32 = jnp.float32
BF16 = jnp.bfloat16
NT = (((1,), (1,)), ((), ()))
TN = (((0,), (0,)), ((), ()))


def iota(shape, dim):
    return lax.broadcasted_iota(jnp.int32, shape, dim)


def halves(x):
    high = x.astype(BF16)
    return high, (x - high.astype(F32)).astype(BF16)


def side(x):
    return jnp.concatenate(halves(x), axis=1)


def mm(a, b, dims=None):
    if dims is None:
        return jnp.dot(a, b, preferred_element_type=F32)
    return lax.dot_general(a, b, dims, preferred_element_type=F32)


def fold(x):
    return x[:, :LANES] + x[:, LANES:]


def feeder_hot(rows, steps, count):
    label = jnp.broadcast_to(rows[:, steps : steps + 1], (rows.shape[0], count))
    lane = iota((rows.shape[0], count), 1).astype(F32)
    return jnp.where(label == lane + 1.0, 1.0, 0.0).astype(BF16)


def split_matrices(kkt_ref, mat_ref):
    arch_count, steps, _ = kkt_ref.shape
    mat_ref[...] = jnp.zeros_like(mat_ref)
    for a in range(arch_count):
        high, low = halves(kkt_ref[a])
        mat_ref[a, 0:steps, 0:steps] = high
        mat_ref[a, LANES : LANES + steps, 0:steps] = low


def apply_matrix(x, matrix):
    count = x.shape[0]
    both = mm(jnp.concatenate(halves(x), axis=0), matrix, NT)
    return both[:count, :LANES] + (both[count:, :LANES] + both[:count, LANES:])


def each_group(offs_ref, arch_count, biggest, step):
    @pl.when(biggest <= WIN)
    def _():
        for a in range(arch_count):
            step(a, pl.multiple_of(offs_ref[0, a], 8))

    @pl.when(biggest > WIN)
    def _():
        def group(a, carry):
            start = offs_ref[0, a]

            def part(t, inner):
                step(a, pl.multiple_of(start + t * WIN, 8))
                return inner

            return lax.fori_loop(0, (offs_ref[1, a] + WIN - 1) // WIN, part, carry)

        lax.fori_loop(0, arch_count, group, 0)


def first_kernel(
    counts_ref, arch_ref, feeder_ref, load_ref, kkt_ref, duals_ref,
    y_ref, pos_ref, offs_ref, sums_ref,
    xt_ref, xs_ref, z_ref, r_ref, mat_ref, offs_smem,
):
    steps, rows_count = load_ref.shape
    arch_count = kkt_ref.shape[0]
    block_total = counts_ref.shape[1]
    feeders = duals_ref.shape[0]
    owned = feeders // block_total
    seg = rows_count // block_total
    lane = iota((1, rows_count), 1)
    bound = jnp.zeros((1, rows_count), jnp.int32)
    base = jnp.zeros((1, rows_count), jnp.int32)
    for k in range(block_total):
        inside = lane >= k * seg
        bound = jnp.where(inside, k * seg + counts_ref[0, k], bound)
        base = jnp.where(inside, k * owned, base)
    live = lane < bound
    kind = jnp.where(live, arch_ref[...], -1)
    label = jnp.where(live, lax.rem(feeder_ref[...], owned) + base + 1, 0).astype(F32)

    chunk = 256
    before = jnp.where(iota((chunk, chunk), 0) < iota((chunk, chunk), 1), 1.0, 0.0).astype(BF16)
    arch_iota = iota((arch_count, chunk), 0)
    carry = jnp.zeros((arch_count, 1), F32)
    hots, ranks = [], []
    for c in range(rows_count // chunk):
        hot = jnp.where(kind[:, c * chunk : (c + 1) * chunk] == arch_iota, 1.0, 0.0)
        ranks.append(mm(hot.astype(BF16), before) + carry)
        hots.append(hot)
        carry = carry + jnp.sum(hot, axis=1, keepdims=True)
    eights = jnp.floor((carry + 7.0) * 0.125)
    lower = jnp.where(iota((arch_count, arch_count), 1) < iota((arch_count, arch_count), 0), 1.0, 0.0).astype(BF16)
    offs = mm(lower, jnp.broadcast_to(eights, (arch_count, LANES)).astype(BF16)) * 8.0
    for c in range(rows_count // chunk):
        part = slice(c * chunk, (c + 1) * chunk)
        place = jnp.sum(hots[c] * (ranks[c] + offs[:, :1]), axis=0, keepdims=True)
        pos_ref[:, part] = jnp.where(live[:, part], place, -1.0).astype(jnp.int32)
    diagonal = iota((arch_count, LANES), 0) == iota((arch_count, LANES), 1)
    offs_row = jnp.sum(jnp.where(diagonal, offs, 0.0), axis=0, keepdims=True).astype(jnp.int32)
    size_row = jnp.sum(jnp.where(diagonal, jnp.broadcast_to(carry, (arch_count, LANES)), 0.0), axis=0, keepdims=True).astype(jnp.int32)
    offs_ref[...] = jnp.zeros_like(offs_ref)
    offs_ref[0:1, :] = offs_row
    offs_ref[1:2, :] = size_row
    biggest = jnp.max(carry).astype(jnp.int32)
    offs_ref[2:3, :] = jnp.full((1, LANES), biggest, jnp.int32)
    pltpu.sync_copy(offs_ref, offs_smem)

    split_matrices(kkt_ref, mat_ref)

    for c in range(rows_count // LANES):
        part = slice(c * LANES, (c + 1) * LANES)
        extra = jnp.where(iota((LANES - steps, LANES), 0) == 0, label[:, part], 0.0)
        block = jnp.concatenate([load_ref[:, part], extra], axis=0).T
        xt_ref[part, :] = side(block)

    duals_side = side(duals_ref[...])

    def permute(b, inner):
        at = pl.multiple_of(b * ROWS, ROWS)
        total = jnp.zeros((ROWS, 2 * LANES), F32)
        for c in range(rows_count // 512):
            part = slice(c * 512, (c + 1) * 512)
            hot = jnp.where(pos_ref[:, part] == iota((ROWS, 512), 0) + at, 1.0, 0.0).astype(BF16)
            total = total + mm(hot, xt_ref[part, :])
        xs = fold(total)
        xs_ref[pl.ds(at, ROWS), :] = xs
        z_ref[pl.ds(at, ROWS), :] = xs - fold(mm(feeder_hot(xs, steps, feeders), duals_side))
        r_ref[pl.ds(at, ROWS), :] = jnp.zeros((ROWS, LANES), F32)
        y_ref[pl.ds(at, ROWS), :] = jnp.zeros((ROWS, LANES), F32)
        return inner

    lax.fori_loop(0, xs_ref.shape[0] // ROWS, permute, 0)

    is_label = iota((WIN, LANES), 1) == steps

    def group(a, row):
        here = pl.ds(row, WIN)
        xs = xs_ref[here, :]
        matrix = mat_ref[a]
        r = apply_matrix(z_ref[here, :], matrix)
        r_ref[here, :] = r
        y = apply_matrix(xs + rho_weight * r, matrix)
        y_ref[here, :] = jnp.where(is_label, xs, y)

    each_group(offs_smem, arch_count, offs_smem[2, 0], group)

    def gather(b, total):
        at = pl.multiple_of(b * ROWS, ROWS)
        here = pl.ds(at, ROWS)
        row = iota((ROWS, LANES), 0) + at
        member = jnp.where((row >= offs_row) & (row < offs_row + size_row), 1.0, 0.0).astype(BF16)
        y = y_ref[here, :]
        right = jnp.concatenate([*halves(r_ref[here, :]), *halves(y), member], axis=1)
        return total + mm(feeder_hot(y, steps, feeders), right, TN)

    sums = lax.fori_loop(0, xs_ref.shape[0] // ROWS, gather, jnp.zeros((feeders, 5 * LANES), F32))
    sums_ref[:, 0:LANES] = sums[:, 0:LANES] + sums[:, LANES : 2 * LANES]
    sums_ref[:, LANES : 2 * LANES] = sums[:, 2 * LANES : 3 * LANES] + sums[:, 3 * LANES : 4 * LANES]
    sums_ref[:, 2 * LANES :] = sums[:, 4 * LANES :]


def middle_kernel(steps, arch_count, sums_ref, duals_ref, pack_ref, next_ref, rest_ref):
    total = sums_ref[0]
    for d in range(1, sums_ref.shape[0]):
        total = total + sums_ref[d]
    loads = total[:, :LANES]
    duals = duals_ref[...]
    cap = duals[:, steps : steps + 1]
    lane = iota(duals.shape, 1)
    after = jnp.maximum(duals + dual_rate * (loads - cap), 0.0)
    after = jnp.where(lane < steps, after, jnp.where(lane == steps, 1.0, 0.0))
    next_ref[...] = after
    rest_ref[...] = total[:, LANES:]
    mixed = lax.dot_general(
        total[:, 2 * LANES :], after, TN, precision=lax.Precision.HIGHEST, preferred_element_type=F32
    )
    pack_ref[0:arch_count, :] = mixed[:arch_count]
    row = iota((8, LANES), 0)
    load_sum = jnp.sum(loads, axis=0, keepdims=True)
    rest_sum = jnp.sum(total[:, LANES : 2 * LANES], axis=0, keepdims=True)
    pack_ref[arch_count:, :] = jnp.where(row == 0, load_sum, jnp.where(row == 1, rest_sum, 0.0))


def last_kernel(
    inv_root, owned, own_ref, offs_ref, y_ref, pos_ref, duals_ref, first_ref, rest_ref, left_ref, right_ref, kkt_ref, target_ref,
    out_ref, feeder_ref, balance_ref,
    z_ref, r_ref, side_ref, mat_ref, target_pad,
):
    arch_count, steps, _ = kkt_ref.shape
    rows_count = pos_ref.shape[1]
    feeders = duals_ref.shape[0]
    split_matrices(kkt_ref, mat_ref)
    pack = left_ref[...] + right_ref[...]
    target_pad[...] = jnp.zeros_like(target_pad)
    target_pad[0:1, 0:steps] = target_ref[...]
    target = target_pad[0:1, :]
    balance = balance_rate * (pack[arch_count : arch_count + 1] * inv_root - target)
    mixed = pack[:arch_count]
    mixed = mixed + mixed[:, steps : steps + 1] * balance
    duals_all = duals_ref[...] + balance
    duals_side = side(duals_all)
    own = pl.ds(pl.multiple_of(own_ref[0] * owned, owned), owned)
    own_before = duals_ref[own, :]
    own_duals = own_before + balance
    own_rest = rest_ref[own, :]

    def pick(b, inner):
        here = pl.ds(pl.multiple_of(b * ROWS, ROWS), ROWS)
        z_ref[here, :] = fold(mm(feeder_hot(y_ref[here, :], steps, feeders), duals_side))
        r_ref[here, :] = jnp.zeros((ROWS, LANES), F32)
        return inner

    lax.fori_loop(0, y_ref.shape[0] // ROWS, pick, 0)

    def group(a, row):
        here = pl.ds(row, WIN)
        r_ref[here, :] = y_ref[here, :] - apply_matrix(z_ref[here, :], mat_ref[a])

    each_group(offs_ref, arch_count, offs_ref[2, 0], group)

    acc = jnp.zeros((EXTRA, LANES), F32)
    first = iota((EXTRA - owned, LANES), 0) == 0
    for a in range(arch_count):
        rows = own_rest[:, LANES + a : LANES + a + 1] * own_duals
        more = jnp.where(first, mixed[a : a + 1], 0.0)
        acc = acc + apply_matrix(jnp.concatenate([rows, more], axis=0), mat_ref[a])

    loads = own_rest[:, :LANES] - acc[:owned]
    cap = first_ref[own, :][:, steps : steps + 1]
    after = jnp.maximum(own_before + dual_rate * (loads - cap), 0.0)
    feeder_ref[...] = after[:, :steps]
    system = pack[arch_count + 1 : arch_count + 2] - acc[owned : owned + 1]
    balance_ref[...] = (balance + balance_rate * (system * inv_root - target))[:, :steps]

    def split_rows(b, inner):
        here = pl.ds(pl.multiple_of(b * ROWS, ROWS), ROWS)
        side_ref[here, :] = side(r_ref[here, :])
        return inner

    lax.fori_loop(0, y_ref.shape[0] // ROWS, split_rows, 0)

    spread_rows = y_ref.shape[0]
    for c in range(rows_count // LANES):
        part = slice(c * LANES, (c + 1) * LANES)
        place = jnp.broadcast_to(pos_ref[:, part].astype(F32), (LANES, LANES)).T.astype(jnp.int32)
        total = jnp.zeros((LANES, 2 * LANES), F32)
        for k in range(spread_rows // 512):
            hot = jnp.concatenate(
                [
                    jnp.where(place == iota((LANES, LANES), 1) + (k * 512 + q * LANES), 1.0, 0.0).astype(BF16)
                    for q in range(4)
                ],
                axis=1,
            )
            total = total + mm(hot, side_ref[k * 512 : (k + 1) * 512, :])
        out_ref[:, part] = fold(total).T[:steps]


def vmem():
    return pl.BlockSpec(memory_space=pltpu.VMEM)


def smem():
    return pl.BlockSpec(memory_space=pltpu.SMEM)


def params():
    return pltpu.CompilerParams(vmem_limit_bytes=VMEM_BYTES)


def on_device(
    load_base, kkt_inverse, archetype, feeder, live_counts, feeder_cap, dual_start, balance_target
):
    steps, rows_count = load_base.shape
    arch_count = kkt_inverse.shape[0]
    block_total = lax.axis_size("dw")
    region_total = lax.axis_size("reg")
    owned = dual_start.shape[0]
    feeders = owned * block_total
    inv_root = 1.0 / math.sqrt(rows_count * block_total * region_total)
    space = -(-(rows_count + 7 * arch_count + WIN) // 512) * 512
    shape = jax.ShapeDtypeStruct

    cap = feeder_cap.astype(F32) * 0.001
    mine = jnp.concatenate(
        [dual_start, cap[:, None], jnp.zeros((owned, LANES - steps - 1), F32)], axis=1
    )
    duals = lax.all_gather(mine, "dw", axis=0, tiled=True)

    y, pos, offs, sums = pl.pallas_call(
        first_kernel,
        name="first",
        in_specs=[smem(), vmem(), vmem(), vmem(), vmem(), vmem()],
        out_specs=[vmem()] * 4,
        out_shape=[
            shape((space, LANES), F32),
            shape((1, rows_count), jnp.int32),
            shape((8, LANES), jnp.int32),
            shape((feeders, 3 * LANES), F32),
        ],
        scratch_shapes=[
            pltpu.VMEM((rows_count, 2 * LANES), BF16),
            pltpu.VMEM((space, LANES), F32),
            pltpu.VMEM((space, LANES), F32),
            pltpu.VMEM((space, LANES), F32),
            pltpu.VMEM((arch_count, 2 * LANES, LANES), BF16),
            pltpu.SMEM((8, LANES), jnp.int32),
        ],
        compiler_params=params(),
    )(
        live_counts,
        archetype.reshape(1, rows_count),
        feeder.reshape(1, rows_count),
        load_base,
        kkt_inverse,
        duals,
    )
    gathered = lax.all_gather(sums, "dw", axis=0)
    pack, next_duals, rest = pl.pallas_call(
        lambda *refs: middle_kernel(steps, arch_count, *refs),
        name="middle",
        in_specs=[vmem()] * 2,
        out_specs=[vmem()] * 3,
        out_shape=[
            shape((arch_count + 8, LANES), F32),
            shape((feeders, LANES), F32),
            shape((feeders, 2 * LANES), F32),
        ],
        compiler_params=params(),
    )(gathered, duals)
    stride = 1
    other = jnp.zeros_like(pack)
    while stride < region_total:
        if stride > 1:
            pack = pack + other
        other = lax.ppermute(pack, "reg", [(i, i ^ stride) for i in range(region_total)])
        stride *= 2
    own = lax.axis_index("dw").astype(jnp.int32).reshape(1)
    out, feeder_duals, balance_dual = pl.pallas_call(
        lambda *refs: last_kernel(inv_root, owned, *refs),
        name="last",
        in_specs=[smem(), smem()] + [vmem()] * 9,
        out_specs=[vmem()] * 3,
        out_shape=[
            shape((steps, rows_count), F32),
            shape((owned, steps), F32),
            shape((1, steps), F32),
        ],
        scratch_shapes=[
            pltpu.VMEM((space, LANES), F32),
            pltpu.VMEM((space, LANES), F32),
            pltpu.VMEM((space, 2 * LANES), BF16),
            pltpu.VMEM((arch_count, 2 * LANES, LANES), BF16),
            pltpu.VMEM((8, LANES), F32),
        ],
        compiler_params=params(),
    )(
        own, offs, y, pos, next_duals, duals, rest, pack, other, kkt_inverse,
        balance_target.reshape(1, steps),
    )
    return (out, feeder_duals, balance_dual.reshape(steps))


def solution(mesh):
    in_specs = (
        P(None, ("scen", "dw", "reg")),
        P(),
        P(("scen", "dw", "reg")),
        P(("scen", "dw", "reg")),
        P(("scen", "dw", "reg"), None),
        P(("scen", "dw", "reg")),
        P(("scen", "dw", "reg"), None),
        P("scen"),
    )
    out_specs = (P(None, ("scen", "dw", "reg")), P(("scen", "dw", "reg"), None), P("scen"))
    return jax.shard_map(
        on_device, mesh=mesh, in_specs=in_specs, out_specs=out_specs, check_vma=False
    )
```

```python
import math

import jax
import jax.numpy as jnp
from jax import lax
from jax.experimental import pallas as pl
from jax.experimental.pallas import tpu as pltpu
from jax.sharding import PartitionSpec as P

rho_weight = 0.5
dual_rate = 0.1
balance_rate = 1.0

LANES = 128
ROWS = 256
WIN = 48
EXTRA = 32
VMEM_BYTES = 24 * 1024 * 1024

F32 = jnp.float32
BF16 = jnp.bfloat16
NT = (((1,), (1,)), ((), ()))
TN = (((0,), (0,)), ((), ()))


def iota(shape, dim):
    return lax.broadcasted_iota(jnp.int32, shape, dim)


def halves(x):
    high = x.astype(BF16)
    return high, (x - high.astype(F32)).astype(BF16)


def side(x):
    return jnp.concatenate(halves(x), axis=1)


def mm(a, b, dims=None):
    if dims is None:
        return jnp.dot(a, b, preferred_element_type=F32)
    return lax.dot_general(a, b, dims, preferred_element_type=F32)


def fold(x):
    return x[:, :LANES] + x[:, LANES:]


def feeder_hot(rows, steps, count):
    label = jnp.broadcast_to(rows[:, steps : steps + 1], (rows.shape[0], count))
    lane = iota((rows.shape[0], count), 1).astype(F32)
    return jnp.where(label == lane + 1.0, 1.0, 0.0).astype(BF16)


def weights(kkt_ref, a):
    high, low = halves(kkt_ref[a])
    steps = kkt_ref.shape[1]
    gap = jnp.zeros((LANES - steps, steps), BF16)
    return jnp.concatenate([high, gap, low, gap], axis=0)


def apply_matrix(x, matrix):
    count = x.shape[0]
    x = x[:, : matrix.shape[1]]
    rest = x - x.astype(BF16).astype(F32)
    both = mm(jnp.concatenate([x, rest], axis=0).astype(BF16), matrix, NT)
    return both[:count, :LANES] + (both[count:, :LANES] + both[:count, LANES:])


def each_group(offs_ref, arch_count, step):
    for a in range(arch_count):
        step(a, pl.multiple_of(offs_ref[0, a], 8), None)

    @pl.when(offs_ref[2, 0] > WIN)
    def _():
        def group(a, carry):
            start = offs_ref[0, a]
            size = (offs_ref[1, a] + 7) // 8 * 8

            def part(t, inner):
                step(a, pl.multiple_of(start + t * WIN, 8), size - t * WIN)
                return inner

            return lax.fori_loop(1, (size + WIN - 1) // WIN, part, carry)

        lax.fori_loop(0, arch_count, group, 0)


def tiers(most):
    return [t for t in (6, 7, 8) if t < most] + [most]


def put(ref, here, value, limit):
    if limit is not None:
        value = jnp.where(iota((WIN, LANES), 0) < limit, value, ref[here, :])
    ref[here, :] = value


def clear_after(offs_ref, refs):
    for t in range(-(-ROWS // WIN)):
        here = pl.ds(pl.multiple_of(offs_ref[3, 0] + t * WIN, 8), WIN)
        for ref in refs:
            ref[here, :] = jnp.zeros((WIN, LANES), F32)


def sort_kernel(
    counts_hbm, arch_hbm, feeder_hbm, load_hbm,
    xs_ref, pos_ref, offs_ref,
    arch_ref, feeder_ref, load_ref, counts_ref, xt_ref, sems, owned, arch_count,
):
    copies = [
        pltpu.make_async_copy(a, b, sems.at[i])
        for i, (a, b) in enumerate(
            [(arch_hbm, arch_ref), (feeder_hbm, feeder_ref), (load_hbm, load_ref), (counts_hbm, counts_ref)]
        )
    ]
    for copy in copies:
        copy.start()
    steps, rows_count = load_ref.shape
    block_total = counts_ref.shape[1]
    seg = rows_count // block_total
    copies[3].wait()
    copies[0].wait()
    copies[1].wait()
    lane = iota((1, rows_count), 1)
    bound = jnp.zeros((1, rows_count), jnp.int32)
    base = jnp.zeros((1, rows_count), jnp.int32)
    for k in range(block_total):
        inside = lane >= k * seg
        bound = jnp.where(inside, k * seg + counts_ref[0, k], bound)
        base = jnp.where(inside, k * owned, base)
    live = lane < bound
    kind = jnp.where(live, arch_ref[...], -1)
    label = jnp.where(live, lax.rem(feeder_ref[...], owned) + base + 1, 0).astype(F32)

    chunk = 256
    before = jnp.where(iota((chunk, chunk), 0) < iota((chunk, chunk), 1), 1.0, 0.0).astype(BF16)
    arch_iota = iota((arch_count, chunk), 0)
    carry = jnp.zeros((arch_count, 1), F32)
    hots, ranks = [], []
    for c in range(rows_count // chunk):
        hot = jnp.where(kind[:, c * chunk : (c + 1) * chunk] == arch_iota, 1.0, 0.0)
        ranks.append(mm(hot.astype(BF16), before) + carry)
        hots.append(hot)
        carry = carry + jnp.sum(hot, axis=1, keepdims=True)
    eights = jnp.floor((carry + 7.0) * 0.125)
    lower = jnp.where(iota((arch_count, arch_count), 1) < iota((arch_count, arch_count), 0), 1.0, 0.0).astype(BF16)
    offs = mm(lower, jnp.broadcast_to(eights, (arch_count, LANES)).astype(BF16)) * 8.0
    for c in range(rows_count // chunk):
        part = slice(c * chunk, (c + 1) * chunk)
        place = jnp.sum(hots[c] * (ranks[c] + offs[:, :1]), axis=0, keepdims=True)
        pos_ref[:, part] = jnp.where(live[:, part], place, -1.0).astype(jnp.int32)
    diagonal = iota((arch_count, LANES), 0) == iota((arch_count, LANES), 1)
    offs_row = jnp.sum(jnp.where(diagonal, offs, 0.0), axis=0, keepdims=True)
    size_row = jnp.sum(jnp.where(diagonal, jnp.broadcast_to(carry, (arch_count, LANES)), 0.0), axis=0, keepdims=True)
    used = (jnp.sum(eights) * 8.0).astype(jnp.int32)
    blocks = (used + ROWS - 1) // ROWS
    row = iota((8, LANES), 0)
    table = jnp.where(row == 0, offs_row, jnp.where(row == 1, size_row, 0.0)).astype(jnp.int32)
    biggest = jnp.max(carry).astype(jnp.int32)
    offs_ref[...] = jnp.where(row == 2, biggest, jnp.where(row == 3, used, jnp.where(row == 4, blocks, table)))

    copies[2].wait()
    for c in range(rows_count // LANES):
        part = slice(c * LANES, (c + 1) * LANES)
        extra = jnp.where(iota((LANES - steps, LANES), 0) == 0, label[:, part], 0.0)
        block = jnp.concatenate([load_ref[:, part], extra], axis=0).T
        xt_ref[part, :] = side(block)

    def permute(b, inner):
        at = pl.multiple_of(b * ROWS, ROWS)
        total = jnp.zeros((ROWS, 2 * LANES), F32)
        for c in range(rows_count // 512):
            part = slice(c * 512, (c + 1) * 512)
            hot = jnp.where(pos_ref[:, part] - at == iota((ROWS, 512), 0), 1.0, 0.0).astype(BF16)
            total = total + mm(hot, xt_ref[part, :])
        xs_ref[pl.ds(at, ROWS), :] = fold(total)
        return inner

    lax.fori_loop(0, blocks, permute, 0)


def first_kernel(
    block_total, own_ref, cap_ref, offs_vmem, xs_ref, kkt_ref, *rest
):
    piece_refs = rest[:-8]
    y_ref, sums_ref, duals_out, z_ref, r_ref, duals_ref, offs_ref, sem = rest[-8:]
    copy = pltpu.make_async_copy(offs_vmem, offs_ref, sem)
    copy.start()
    arch_count = kkt_ref.shape[0]
    steps = piece_refs[0].shape[1]
    feeders = duals_ref.shape[0]
    owned = feeders // block_total
    own = own_ref[0]
    spare = LANES - steps
    duals_ref[...] = jnp.zeros_like(duals_ref)
    if len(piece_refs) == 1:
        duals_ref[:, 0:steps] = piece_refs[0][...]
    else:
        for p, ref in enumerate(piece_refs):
            duals_ref[pl.ds(pl.multiple_of((own ^ p) * owned, owned), owned), 0:steps] = ref[...]
    duals = duals_ref[...]
    duals_out[...] = duals
    duals_side = side(duals)
    blocks = jnp.max(offs_vmem[4:5, :])

    def pick(b, inner):
        here = pl.ds(pl.multiple_of(b * ROWS, ROWS), ROWS)
        xs = xs_ref[here, :]
        z_ref[here, :] = xs - fold(mm(feeder_hot(xs, steps, feeders), duals_side))
        return inner

    lax.fori_loop(0, blocks, pick, 0)
    copy.wait()

    is_label = iota((WIN, LANES), 1) == steps

    def group(a, row, limit):
        here = pl.ds(row, WIN)
        xs = xs_ref[here, :]
        matrix = weights(kkt_ref, a)
        r = apply_matrix(z_ref[here, :], matrix)
        put(r_ref, here, r, limit)
        y = apply_matrix(xs + rho_weight * r, matrix)
        put(y_ref, here, jnp.where(is_label, xs, y), limit)

    each_group(offs_ref, arch_count, group)
    clear_after(offs_ref, [r_ref, y_ref])

    offs_row = offs_vmem[0:1, :]
    size_row = offs_vmem[1:2, :]

    def gather(b, total):
        at = pl.multiple_of(b * ROWS, ROWS)
        here = pl.ds(at, ROWS)
        row = iota((ROWS, LANES), 0) + at
        member = jnp.where((row >= offs_row) & (row < offs_row + size_row), 1.0, 0.0).astype(BF16)
        y = y_ref[here, :]
        right = jnp.concatenate([*halves(r_ref[here, :]), *halves(y), member], axis=1)
        return total + mm(feeder_hot(y, steps, feeders), right, TN)

    sums = lax.fori_loop(0, blocks, gather, jnp.zeros((feeders, 5 * LANES), F32))
    loads = sums[:, 0:LANES] + sums[:, LANES : 2 * LANES]
    others = sums[:, 2 * LANES : 3 * LANES] + sums[:, 3 * LANES : 4 * LANES]
    counts = sums[:, 4 * LANES :]
    low = jnp.concatenate([counts[:, spare : spare + steps], counts[:, 0:spare]], axis=1)
    high = jnp.concatenate([counts[:, 2 * spare : LANES], counts[:, 0 : 2 * spare]], axis=1)
    lane = iota((feeders, LANES), 1)
    sums_ref[0:feeders, 0:LANES] = jnp.where(lane < steps, loads, low)
    sums_ref[0:feeders, LANES:] = jnp.where(lane < steps, others, high)
    row = iota((8, LANES), 0)
    sums_ref[feeders:, 0:LANES] = jnp.where(row == 0, jnp.sum(loads, axis=0, keepdims=True), 0.0)
    sums_ref[feeders:, LANES:] = jnp.where(row == 0, jnp.sum(others, axis=0, keepdims=True), 0.0)
    mine = pl.ds(pl.multiple_of(own * owned, owned), owned)
    place = iota((owned, LANES), 0)
    cap = jnp.zeros((owned, LANES), jnp.int32)
    for q in range(owned):
        cap = jnp.where(place == q, cap_ref[q], cap)
    cap = jnp.where(iota((owned, LANES), 1) < steps, cap.astype(F32) * 0.001, 0.0)
    sums_ref[mine, 0:LANES] = sums_ref[mine, 0:LANES] - cap


def middle_kernel(steps, arch_count, sums_ref, duals_ref, pack_ref, next_ref, rest_ref):
    total = sums_ref[0]
    for d in range(1, sums_ref.shape[0]):
        total = total + sums_ref[d]
    feeders = duals_ref.shape[0]
    spare = LANES - steps
    excess = total[:feeders, :LANES]
    others = total[:feeders, LANES:]
    lane = iota((feeders, LANES), 1)
    after = jnp.maximum(duals_ref[...] + dual_rate * excess, 0.0)
    after = jnp.where(lane < steps, after, jnp.where(lane == steps, 1.0, 0.0))
    next_ref[...] = after
    counts = jnp.concatenate([excess[:, steps:], others[:, steps:], jnp.zeros((feeders, LANES - 2 * spare), F32)], axis=1)
    rest_ref[:, :LANES] = others
    rest_ref[:, LANES:] = counts
    mixed = lax.dot_general(counts, after, TN, precision=lax.Precision.HIGHEST, preferred_element_type=F32)
    pack_ref[0:arch_count, :] = mixed[:arch_count]
    row = iota((8, LANES), 0)
    pack_ref[arch_count:, :] = jnp.where(
        row == 0, total[feeders : feeders + 1, :LANES], jnp.where(row == 1, total[feeders : feeders + 1, LANES:], 0.0)
    )


def last_kernel(
    inv_root, owned, own_ref, cap_ref, offs_vmem, y_ref, pos_ref, duals_ref, rest_ref, left_ref, right_ref, kkt_ref, target_ref,
    out_ref, feeder_ref, balance_ref,
    z_ref, r_ref, side_ref, acc_ref, target_pad, offs_ref, sem,
):
    copy = pltpu.make_async_copy(offs_vmem, offs_ref, sem)
    copy.start()
    arch_count = kkt_ref.shape[0]
    steps = target_ref.shape[1]
    rows_count = pos_ref.shape[1]
    feeders = duals_ref.shape[0]
    pack = left_ref[...] + right_ref[...]
    target_pad[...] = jnp.zeros_like(target_pad)
    target_pad[0:1, 0:steps] = target_ref[...]
    target = target_pad[0:1, :]
    balance = balance_rate * (pack[arch_count : arch_count + 1] * inv_root - target)
    mixed = pack[:arch_count]
    mixed = mixed + mixed[:, steps : steps + 1] * balance
    duals_all = duals_ref[...] + balance
    duals_side = side(duals_all)
    own = pl.ds(pl.multiple_of(own_ref[0] * owned, owned), owned)
    own_before = duals_ref[own, :]
    own_duals = own_before + balance
    own_rest = rest_ref[own, :]
    blocks = jnp.max(offs_vmem[4:5, :])

    def pick(b, inner):
        here = pl.ds(pl.multiple_of(b * ROWS, ROWS), ROWS)
        z_ref[here, :] = fold(mm(feeder_hot(y_ref[here, :], steps, feeders), duals_side))
        return inner

    lax.fori_loop(0, blocks, pick, 0)
    copy.wait()

    first = iota((EXTRA - owned, LANES), 0) == 0
    acc_ref[...] = jnp.zeros_like(acc_ref)

    def group(a, row, limit):
        here = pl.ds(row, WIN)
        matrix = weights(kkt_ref, a)
        if limit is not None:
            put(r_ref, here, y_ref[here, :] - apply_matrix(z_ref[here, :], matrix), limit)
            return
        rows = own_rest[:, LANES + a : LANES + a + 1] * own_duals
        more = jnp.where(first, mixed[a : a + 1], 0.0)
        done = apply_matrix(jnp.concatenate([z_ref[here, :], rows, more], axis=0), matrix)
        r_ref[here, :] = y_ref[here, :] - done[:WIN]
        acc_ref[...] += done[WIN:]

    each_group(offs_ref, arch_count, group)
    clear_after(offs_ref, [r_ref])
    acc = acc_ref[...]

    loads = own_rest[:, :LANES] - acc[:owned]
    place = iota((owned, LANES), 0)
    cap = jnp.zeros((owned, LANES), jnp.int32)
    for q in range(owned):
        cap = jnp.where(place == q, cap_ref[q], cap)
    after = jnp.maximum(own_before + dual_rate * (loads - cap.astype(F32) * 0.001), 0.0)
    feeder_ref[...] = after[:, :steps]
    system = pack[arch_count + 1 : arch_count + 2] - acc[owned : owned + 1]
    balance_ref[...] = (balance + balance_rate * (system * inv_root - target))[:, :steps]

    def split_rows(b, inner):
        here = pl.ds(pl.multiple_of(b * ROWS, ROWS), ROWS)
        side_ref[here, :] = side(r_ref[here, :])
        return inner

    lax.fori_loop(0, blocks, split_rows, 0)

    def spread(reach):
        def columns(c, inner):
            part = pl.ds(pl.multiple_of(c * 256, 256), 256)
            place = jnp.broadcast_to(pos_ref[:, part].astype(F32), (LANES, 256)).T.astype(jnp.int32)
            hot = jnp.concatenate(
                [
                    jnp.where(place == iota((256, LANES), 1) + q * LANES, 1.0, 0.0).astype(BF16)
                    for q in range(reach * ROWS // LANES)
                ],
                axis=1,
            )
            out_ref[:, part] = fold(mm(hot, side_ref[0 : reach * ROWS, :])).T[:steps]
            return inner

        lax.fori_loop(0, rows_count // 256, columns, 0)

    count = blocks
    low = 0
    for reach in tiers(y_ref.shape[0] // ROWS):
        @pl.when((count > low) & (count <= reach))
        def _():
            def clear(b, inner):
                here = pl.ds(pl.multiple_of(b * ROWS, ROWS), ROWS)
                side_ref[here, :] = jnp.zeros((ROWS, 2 * LANES), BF16)
                return inner

            lax.fori_loop(count, reach, clear, 0)
            spread(reach)

        low = reach


def vmem():
    return pl.BlockSpec(memory_space=pltpu.VMEM)


def smem():
    return pl.BlockSpec(memory_space=pltpu.SMEM)


def hbm():
    return pl.BlockSpec(memory_space=pltpu.HBM)


def stay(x):
    return pltpu.with_memory_space_constraint(x, pltpu.HBM)


def params():
    return pltpu.CompilerParams(vmem_limit_bytes=VMEM_BYTES)


def cost(flops):
    return pl.CostEstimate(flops=flops, transcendentals=0, bytes_accessed=8 * 1024 * 1024)


def exchange(x, axis, mask):
    return lax.ppermute(x, axis, [(i, i ^ mask) for i in range(lax.axis_size(axis))])


def on_device(
    load_base, kkt_inverse, archetype, feeder, live_counts, feeder_cap, dual_start, balance_target
):
    steps, rows_count = load_base.shape
    arch_count = kkt_inverse.shape[0]
    block_total = lax.axis_size("dw")
    region_total = lax.axis_size("reg")
    owned = dual_start.shape[0]
    feeders = owned * block_total
    inv_root = 1.0 / math.sqrt(rows_count * block_total * region_total)
    space = -(-(rows_count + 7 * arch_count + ROWS + WIN) // ROWS) * ROWS
    shape = jax.ShapeDtypeStruct
    own = lax.axis_index("dw").astype(jnp.int32).reshape(1)

    if block_total == 4:
        far = exchange(dual_start, "dw", 2)
    xs, pos, offs = pl.pallas_call(
        lambda *refs: sort_kernel(*refs, owned, arch_count),
        name="sort",
        cost_estimate=cost(5 * 10**9),
        in_specs=[hbm()] * 4,
        out_specs=[vmem()] * 3,
        out_shape=[
            pltpu.VMEM((space, LANES), F32),
            pltpu.VMEM((1, rows_count), jnp.int32),
            pltpu.VMEM((8, LANES), jnp.int32),
        ],
        scratch_shapes=[
            pltpu.VMEM((1, rows_count), jnp.int32),
            pltpu.VMEM((1, rows_count), jnp.int32),
            pltpu.VMEM((steps, rows_count), F32),
            pltpu.SMEM((1, block_total), jnp.int32),
            pltpu.VMEM((rows_count, 2 * LANES), BF16),
            pltpu.SemaphoreType.DMA((4,)),
        ],
        compiler_params=params(),
    )(
        stay(live_counts),
        stay(archetype.reshape(1, rows_count)),
        stay(feeder.reshape(1, rows_count)),
        stay(load_base),
    )
    if block_total == 4:
        far, offs = lax.optimization_barrier((far, offs))
        pieces = [dual_start, exchange(dual_start, "dw", 1), far, exchange(far, "dw", 1)]
    else:
        pieces = [lax.all_gather(dual_start, "dw", axis=0, tiled=True)]
    y, sums, duals = pl.pallas_call(
        lambda *refs: first_kernel(block_total, *refs),
        name="first",
        cost_estimate=cost(6 * 10**9),
        in_specs=[smem()] * 2 + [vmem()] * (3 + len(pieces)),
        out_specs=[vmem()] * 3,
        out_shape=[
            pltpu.VMEM((space, LANES), F32),
            shape((feeders + 8, 2 * LANES), F32),
            pltpu.VMEM((feeders, LANES), F32),
        ],
        scratch_shapes=[
            pltpu.VMEM((space, LANES), F32),
            pltpu.VMEM((space, LANES), F32),
            pltpu.VMEM((feeders, LANES), F32),
            pltpu.SMEM((8, LANES), jnp.int32),
            pltpu.SemaphoreType.DMA,
        ],
        compiler_params=params(),
    )(own, feeder_cap, offs, xs, kkt_inverse, *pieces)
    gathered = lax.all_gather(sums, "dw", axis=0)
    pack, next_duals, rest = pl.pallas_call(
        lambda *refs: middle_kernel(steps, arch_count, *refs),
        name="middle",
        in_specs=[vmem()] * 2,
        out_specs=[vmem()] * 3,
        out_shape=[
            shape((arch_count + 8, LANES), F32),
            shape((feeders, LANES), F32),
            shape((feeders, 2 * LANES), F32),
        ],
        compiler_params=params(),
    )(gathered, duals)
    stride = 1
    other = jnp.zeros_like(pack)
    while stride < region_total:
        if stride > 1:
            pack = pack + other
        other = exchange(pack, "reg", stride)
        stride *= 2
    out, feeder_duals, balance_dual = pl.pallas_call(
        lambda *refs: last_kernel(inv_root, owned, *refs),
        name="last",
        cost_estimate=cost(6 * 10**9),
        in_specs=[smem()] * 2 + [vmem()] * 9,
        out_specs=[vmem()] * 3,
        out_shape=[
            shape((steps, rows_count), F32),
            shape((owned, steps), F32),
            shape((1, steps), F32),
        ],
        scratch_shapes=[
            pltpu.VMEM((space, LANES), F32),
            pltpu.VMEM((space, LANES), F32),
            pltpu.VMEM((space, 2 * LANES), BF16),
            pltpu.VMEM((EXTRA, LANES), F32),
            pltpu.VMEM((8, LANES), F32),
            pltpu.SMEM((8, LANES), jnp.int32),
            pltpu.SemaphoreType.DMA,
        ],
        compiler_params=params(),
    )(
        own, feeder_cap, offs, y, pos, next_duals, rest, pack, other, kkt_inverse,
        balance_target.reshape(1, steps),
    )
    return (out, feeder_duals, balance_dual.reshape(steps))


def solution(mesh):
    in_specs = (
        P(None, ("scen", "dw", "reg")),
        P(),
        P(("scen", "dw", "reg")),
        P(("scen", "dw", "reg")),
        P(("scen", "dw", "reg"), None),
        P(("scen", "dw", "reg")),
        P(("scen", "dw", "reg"), None),
        P("scen"),
    )
    out_specs = (P(None, ("scen", "dw", "reg")), P(("scen", "dw", "reg"), None), P("scen"))
    return jax.shard_map(
        on_device, mesh=mesh, in_specs=in_specs, out_specs=out_specs, check_vma=False
    )
```

```python
import math

import jax
import jax.numpy as jnp
from jax import lax
from jax.experimental import pallas as pl
from jax.experimental.pallas import tpu as pltpu
from jax.sharding import PartitionSpec as P

rho_weight = 0.5
dual_rate = 0.1
balance_rate = 1.0

LANES = 128
ROWS = 256
WIN = 48
BLOCKS = 8
EXTRA = 32
VMEM_BYTES = 24 * 1024 * 1024

F32 = jnp.float32
BF16 = jnp.bfloat16
NT = (((1,), (1,)), ((), ()))
TN = (((0,), (0,)), ((), ()))


def iota(shape, dim):
    return lax.broadcasted_iota(jnp.int32, shape, dim)


def halves(x):
    high = x.astype(BF16)
    return high, (x - high.astype(F32)).astype(BF16)


def side(x):
    return jnp.concatenate(halves(x), axis=1)


def mm(a, b, dims=None):
    if dims is None:
        return jnp.dot(a, b, preferred_element_type=F32)
    return lax.dot_general(a, b, dims, preferred_element_type=F32)


def fold(x):
    return x[:, :LANES] + x[:, LANES:]


def feeder_hot(rows, steps, count):
    label = jnp.broadcast_to(rows[:, steps : steps + 1], (rows.shape[0], count))
    lane = iota((rows.shape[0], count), 1).astype(F32)
    return jnp.where(label == lane + 1.0, 1.0, 0.0).astype(BF16)


def weights(kkt_ref, a):
    high, low = halves(kkt_ref[a])
    steps = kkt_ref.shape[1]
    gap = jnp.zeros((LANES - steps, steps), BF16)
    return jnp.concatenate([high, gap, low, gap], axis=0)


def apply_matrix(x, matrix):
    count = x.shape[0]
    x = x[:, : matrix.shape[1]]
    rest = x - x.astype(BF16).astype(F32)
    both = mm(jnp.concatenate([x, rest], axis=0).astype(BF16), matrix, NT)
    return both[:count, :LANES] + (both[count:, :LANES] + both[:count, LANES:])


def each_group(offs_ref, arch_count, step):
    for a in range(arch_count):
        step(a, pl.multiple_of(offs_ref[0, a], 8), None)

    @pl.when(offs_ref[2, 0] > WIN)
    def _():
        def group(a, carry):
            start = offs_ref[0, a]
            size = (offs_ref[1, a] + 7) // 8 * 8

            def part(t, inner):
                step(a, pl.multiple_of(start + t * WIN, 8), size - t * WIN)
                return inner

            return lax.fori_loop(1, (size + WIN - 1) // WIN, part, carry)

        lax.fori_loop(0, arch_count, group, 0)


def tiers(most):
    return [t for t in (6, 7, 8) if t < most] + [most]


def put(ref, here, value, limit):
    if limit is not None:
        value = jnp.where(iota((WIN, LANES), 0) < limit, value, ref[here, :])
    ref[here, :] = value


def clear_after(offs_ref, refs):
    here = pl.ds(pl.multiple_of(offs_ref[3, 0], 8), WIN)
    for ref in refs:
        ref[here, :] = jnp.zeros((WIN, LANES), F32)


def each_block(blocks, step, total):
    for b in range(BLOCKS):
        total = step(b * ROWS, total)

    def more(b, inner):
        return step(pl.multiple_of(b * ROWS, ROWS), inner)

    return lax.fori_loop(BLOCKS, blocks, more, total)


def cap_column(cap_ref):
    owned = cap_ref.shape[1]
    cap = cap_ref[...].astype(F32) * 0.001
    diagonal = iota((owned, owned), 0) == iota((owned, owned), 1)
    return jnp.sum(jnp.where(diagonal, cap, 0.0), axis=1, keepdims=True)


def first_kernel(
    counts_hbm, arch_hbm, feeder_hbm, load_hbm, kkt_hbm, start_ref, cap_ref,
    y_ref, pos_ref, offs_vmem, sums_ref, duals_ref,
    arch_ref, feeder_ref, load_ref, kkt_ref, counts_ref, xt_ref, code_ref, xs_ref, z_ref, r_ref, mat_ref, offs_ref, sems,
):
    copies = [
        pltpu.make_async_copy(a, b, sems.at[i])
        for i, (a, b) in enumerate(
            [(arch_hbm, arch_ref), (feeder_hbm, feeder_ref), (load_hbm, load_ref), (counts_hbm, counts_ref), (kkt_hbm, kkt_ref)]
        )
    ]
    for copy in copies:
        copy.start()
    arch_count, steps, _ = kkt_ref.shape
    feeders = duals_ref.shape[0]
    mat_ref[...] = jnp.zeros_like(mat_ref)
    duals_ref[...] = jnp.zeros_like(duals_ref)
    duals_ref[:, 0:steps] = start_ref[...]
    duals_side = side(duals_ref[...])
    rows_count = load_ref.shape[1]
    block_total = counts_ref.shape[1]
    owned = feeders // block_total
    own = lax.axis_index("dw")
    spare = LANES - steps
    seg = rows_count // block_total
    copies[3].wait()
    copies[0].wait()
    copies[1].wait()
    lane = iota((1, rows_count), 1)
    bound = jnp.zeros((1, rows_count), jnp.int32)
    base = jnp.zeros((1, rows_count), jnp.int32)
    for k in range(block_total):
        inside = lane >= k * seg
        bound = jnp.where(inside, k * seg + counts_ref[0, k], bound)
        base = jnp.where(inside, k * owned, base)
    live = lane < bound
    kind = jnp.where(live, arch_ref[...], -1)
    label = jnp.where(live, lax.rem(feeder_ref[...], owned) + base + 1, 0).astype(F32)

    chunk = 256
    before = jnp.where(iota((chunk, chunk), 0) < iota((chunk, chunk), 1), 1.0, 0.0).astype(BF16)
    arch_iota = iota((arch_count, chunk), 0)
    carry = jnp.zeros((arch_count, 1), F32)
    hots, ranks = [], []
    for c in range(rows_count // chunk):
        hot = jnp.where(kind[:, c * chunk : (c + 1) * chunk] == arch_iota, 1.0, 0.0)
        ranks.append(mm(hot.astype(BF16), before) + carry)
        hots.append(hot)
        carry = carry + jnp.sum(hot, axis=1, keepdims=True)
    eights = jnp.floor((carry + 7.0) * 0.125)
    lower = jnp.where(iota((arch_count, arch_count), 1) < iota((arch_count, arch_count), 0), 1.0, 0.0).astype(BF16)
    offs = mm(lower, jnp.broadcast_to(eights, (arch_count, LANES)).astype(BF16)) * 8.0
    for c in range(rows_count // chunk):
        part = slice(c * chunk, (c + 1) * chunk)
        place = jnp.sum(hots[c] * (ranks[c] + offs[:, :1]), axis=0, keepdims=True)
        place = jnp.where(live[:, part], place, -1.0)
        pos_ref[:, part] = place.astype(jnp.int32)
        block = jnp.floor(place * (1.0 / ROWS))
        within = place - block * ROWS
        code_ref[:, part] = jnp.where(within == iota((ROWS, chunk), 0).astype(F32), block, -1.0).astype(BF16)
    diagonal = iota((arch_count, LANES), 0) == iota((arch_count, LANES), 1)
    offs_row = jnp.sum(jnp.where(diagonal, offs, 0.0), axis=0, keepdims=True)
    size_row = jnp.sum(jnp.where(diagonal, jnp.broadcast_to(carry, (arch_count, LANES)), 0.0), axis=0, keepdims=True)
    used = (jnp.sum(eights) * 8.0).astype(jnp.int32)
    blocks = (used + ROWS - 1) // ROWS
    row = iota((8, LANES), 0)
    table = jnp.where(row == 0, offs_row, jnp.where(row == 1, size_row, 0.0)).astype(jnp.int32)
    biggest = jnp.max(carry).astype(jnp.int32)
    offs_vmem[...] = jnp.where(row == 2, biggest, jnp.where(row == 3, used, jnp.where(row == 4, blocks, table)))
    to_scalar = pltpu.make_async_copy(offs_vmem, offs_ref, sems.at[5])
    to_scalar.start()

    copies[2].wait()
    for c in range(rows_count // LANES):
        part = slice(c * LANES, (c + 1) * LANES)
        extra = jnp.where(iota((LANES - steps, LANES), 0) == 0, label[:, part], 0.0)
        block = jnp.concatenate([load_ref[:, part], extra], axis=0).T
        xt_ref[part, :] = side(block)

    copies[4].wait()
    for a in range(arch_count):
        high, low = halves(kkt_ref[a])
        mat_ref[a, 0:steps, 0:steps] = high
        mat_ref[a, LANES : LANES + steps, 0:steps] = low

    def permute(b, inner):
        at = pl.multiple_of(b * ROWS, ROWS)
        hot = jnp.where(code_ref[...] == b.astype(F32).astype(BF16), 1.0, 0.0).astype(BF16)
        xs_ref[pl.ds(at, ROWS), :] = fold(mm(hot, xt_ref[...]))
        return inner

    lax.fori_loop(0, blocks, permute, 0)

    def pick(at, inner):
        here = pl.ds(at, ROWS)
        xs = xs_ref[here, :]
        z_ref[here, :] = xs - fold(mm(feeder_hot(xs, steps, feeders), duals_side))
        r_ref[here, :] = jnp.zeros((ROWS, LANES), F32)
        y_ref[here, :] = jnp.zeros((ROWS, LANES), F32)
        return inner

    each_block(blocks, pick, 0)
    to_scalar.wait()

    is_label = iota((WIN, LANES), 1) == steps

    def group(a, row, limit):
        here = pl.ds(row, WIN)
        xs = xs_ref[here, :]
        matrix = mat_ref[a]
        r = apply_matrix(z_ref[here, :], matrix)
        put(r_ref, here, r, limit)
        y = apply_matrix(xs + rho_weight * r, matrix)
        put(y_ref, here, jnp.where(is_label, xs, y), limit)

    each_group(offs_ref, arch_count, group)
    clear_after(offs_ref, [r_ref, y_ref])

    offs_row = offs_row.astype(jnp.int32)
    ends_row = offs_row + size_row.astype(jnp.int32)

    def gather(at, total):
        here = pl.ds(at, ROWS)
        row = iota((ROWS, LANES), 0) + at
        member = jnp.where((row >= offs_row) & (row < ends_row), 1.0, 0.0).astype(BF16)
        y = y_ref[here, :]
        right = jnp.concatenate([*halves(r_ref[here, :]), *halves(y), member], axis=1)
        return total + mm(feeder_hot(y, steps, feeders), right, TN)

    sums = each_block(blocks, gather, jnp.zeros((feeders, 5 * LANES), F32))
    loads = sums[:, 0:LANES] + sums[:, LANES : 2 * LANES]
    others = sums[:, 2 * LANES : 3 * LANES] + sums[:, 3 * LANES : 4 * LANES]
    counts = sums[:, 4 * LANES :]
    low = jnp.concatenate([counts[:, spare : spare + steps], counts[:, 0:spare]], axis=1)
    high = jnp.concatenate([counts[:, 2 * spare : LANES], counts[:, 0 : 2 * spare]], axis=1)
    lane = iota((feeders, LANES), 1)
    sums_ref[0:feeders, 0:LANES] = jnp.where(lane < steps, loads, low)
    sums_ref[0:feeders, LANES:] = jnp.where(lane < steps, others, high)
    row = iota((8, LANES), 0)
    sums_ref[feeders:, 0:LANES] = jnp.where(row == 0, jnp.sum(loads, axis=0, keepdims=True), 0.0)
    sums_ref[feeders:, LANES:] = jnp.where(row == 0, jnp.sum(others, axis=0, keepdims=True), 0.0)
    mine = pl.ds(pl.multiple_of(own * owned, owned), owned)
    cap = jnp.where(iota((owned, LANES), 1) < steps, cap_column(cap_ref), 0.0)
    sums_ref[mine, 0:LANES] = sums_ref[mine, 0:LANES] - cap


def middle_kernel(steps, arch_count, sums_ref, duals_ref, pack_ref, next_ref, rest_ref):
    total = sums_ref[0]
    for d in range(1, sums_ref.shape[0]):
        total = total + sums_ref[d]
    feeders = duals_ref.shape[0]
    spare = LANES - steps
    excess = total[:feeders, :LANES]
    others = total[:feeders, LANES:]
    lane = iota((feeders, LANES), 1)
    after = jnp.maximum(duals_ref[...] + dual_rate * excess, 0.0)
    after = jnp.where(lane < steps, after, jnp.where(lane == steps, 1.0, 0.0))
    next_ref[...] = after
    counts = jnp.concatenate([excess[:, steps:], others[:, steps:], jnp.zeros((feeders, LANES - 2 * spare), F32)], axis=1)
    rest_ref[:, :LANES] = others
    rest_ref[:, LANES:] = counts
    mixed = lax.dot_general(counts, after, TN, precision=lax.Precision.HIGHEST, preferred_element_type=F32)
    pack_ref[0:arch_count, :] = mixed[:arch_count]
    row = iota((8, LANES), 0)
    pack_ref[arch_count:, :] = jnp.where(
        row == 0, total[feeders : feeders + 1, :LANES], jnp.where(row == 1, total[feeders : feeders + 1, LANES:], 0.0)
    )


def last_kernel(
    inv_root, cap_ref, offs_vmem, y_ref, pos_ref, duals_ref, rest_ref, left_ref, right_ref, kkt_ref, target_ref,
    out_hbm, feeder_ref, balance_ref,
    z_ref, r_ref, side_ref, acc_ref, target_pad, stage_ref, offs_ref, sem, out_sems,
):
    copy = pltpu.make_async_copy(offs_vmem, offs_ref, sem)
    copy.start()
    arch_count = kkt_ref.shape[0]
    owned = cap_ref.shape[1]
    steps = target_ref.shape[1]
    rows_count = pos_ref.shape[1]
    feeders = duals_ref.shape[0]
    pack = left_ref[...] + right_ref[...]
    target_pad[...] = jnp.zeros_like(target_pad)
    target_pad[0:1, 0:steps] = target_ref[...]
    target = target_pad[0:1, :]
    balance = balance_rate * (pack[arch_count : arch_count + 1] * inv_root - target)
    mixed = pack[:arch_count]
    mixed = mixed + mixed[:, steps : steps + 1] * balance
    duals_all = duals_ref[...] + balance
    duals_side = side(duals_all)
    own = pl.ds(pl.multiple_of(lax.axis_index("dw") * owned, owned), owned)
    own_before = duals_ref[own, :]
    own_duals = own_before + balance
    own_rest = rest_ref[own, :]
    blocks = jnp.max(offs_vmem[4:5, :])

    def pick(at, inner):
        here = pl.ds(at, ROWS)
        z_ref[here, :] = fold(mm(feeder_hot(y_ref[here, :], steps, feeders), duals_side))
        r_ref[here, :] = jnp.zeros((ROWS, LANES), F32)
        return inner

    each_block(blocks, pick, 0)
    copy.wait()

    first = iota((EXTRA - owned, LANES), 0) == 0
    acc_ref[...] = jnp.zeros_like(acc_ref)

    def group(a, row, limit):
        here = pl.ds(row, WIN)
        matrix = weights(kkt_ref, a)
        if limit is not None:
            put(r_ref, here, y_ref[here, :] - apply_matrix(z_ref[here, :], matrix), limit)
            return
        rows = own_rest[:, LANES + a : LANES + a + 1] * own_duals
        more = jnp.where(first, mixed[a : a + 1], 0.0)
        done = apply_matrix(jnp.concatenate([z_ref[here, :], rows, more], axis=0), matrix)
        r_ref[here, :] = y_ref[here, :] - done[:WIN]
        acc_ref[...] += done[WIN:]

    each_group(offs_ref, arch_count, group)
    clear_after(offs_ref, [r_ref])
    acc = acc_ref[...]

    loads = own_rest[:, :LANES] - acc[:owned]
    after = jnp.maximum(own_before + dual_rate * (loads - cap_column(cap_ref)), 0.0)
    feeder_ref[...] = after[:, :steps]
    system = pack[arch_count + 1 : arch_count + 2] - acc[owned : owned + 1]
    balance_ref[...] = (balance + balance_rate * (system * inv_root - target))[:, :steps]

    def columns(c, reach):
        part = pl.ds(pl.multiple_of(c * ROWS, ROWS), ROWS)
        place = pos_ref[:, part].astype(F32)
        block = jnp.floor(place * (1.0 / LANES))
        within = place - block * LANES
        code = jnp.where(within == iota((LANES, ROWS), 0).astype(F32), block, -1.0).T.astype(BF16)
        hot = jnp.concatenate(
            [jnp.where(code == jnp.bfloat16(q), 1.0, 0.0).astype(BF16) for q in range(reach * ROWS // LANES)], axis=1
        )
        stage_ref[:, part] = fold(mm(hot, side_ref[0 : reach * ROWS, :])).T[:steps]
        return pltpu.make_async_copy(stage_ref.at[:, part], out_hbm.at[:, part], out_sems.at[c])

    def spread(reach):
        def pair(c, inner):
            for half in range(2):
                columns(2 * c + half, reach).start()
            return inner

        lax.fori_loop(0, rows_count // (2 * ROWS), pair, 0)

    count = blocks
    low = 0
    for reach in tiers(y_ref.shape[0] // ROWS):
        @pl.when((count > low) & (count <= reach))
        def _():
            for b in range(reach):
                here = slice(b * ROWS, (b + 1) * ROWS)
                side_ref[here, :] = side(r_ref[here, :])
            spread(reach)

        low = reach

    for c in range(rows_count // ROWS):
        part = slice(c * ROWS, (c + 1) * ROWS)
        pltpu.make_async_copy(stage_ref.at[:, part], out_hbm.at[:, part], out_sems.at[c]).wait()


def vmem():
    return pl.BlockSpec(memory_space=pltpu.VMEM)


def hbm():
    return pl.BlockSpec(memory_space=pltpu.HBM)


def stay(x):
    return pltpu.with_memory_space_constraint(x, pltpu.HBM)


def params():
    return pltpu.CompilerParams(vmem_limit_bytes=VMEM_BYTES)


def exchange(x, axis, mask):
    return lax.ppermute(x, axis, [(i, i ^ mask) for i in range(lax.axis_size(axis))])


def on_device(
    load_base, kkt_inverse, archetype, feeder, live_counts, feeder_cap, dual_start, balance_target
):
    steps, rows_count = load_base.shape
    arch_count = kkt_inverse.shape[0]
    block_total = lax.axis_size("dw")
    region_total = lax.axis_size("reg")
    owned = dual_start.shape[0]
    feeders = owned * block_total
    inv_root = 1.0 / math.sqrt(rows_count * block_total * region_total)
    space = -(-(rows_count + 7 * arch_count + ROWS + WIN) // ROWS) * ROWS
    shape = jax.ShapeDtypeStruct
    cap = feeder_cap.reshape(1, owned)
    duals = lax.all_gather(dual_start, "dw", axis=0, tiled=True)
    y, pos, offs, sums, duals = pl.pallas_call(
        first_kernel,
        name="first",
        in_specs=[hbm()] * 5 + [vmem()] * 2,
        out_specs=[vmem()] * 5,
        out_shape=[
            shape((space, LANES), F32),
            shape((1, rows_count), jnp.int32),
            shape((8, LANES), jnp.int32),
            shape((feeders + 8, 2 * LANES), F32),
            shape((feeders, LANES), F32),
        ],
        scratch_shapes=[
            pltpu.VMEM((1, rows_count), jnp.int32),
            pltpu.VMEM((1, rows_count), jnp.int32),
            pltpu.VMEM((steps, rows_count), F32),
            pltpu.VMEM((arch_count, steps, steps), F32),
            pltpu.SMEM((1, block_total), jnp.int32),
            pltpu.VMEM((rows_count, 2 * LANES), BF16),
            pltpu.VMEM((ROWS, rows_count), BF16),
            pltpu.VMEM((space, LANES), F32),
            pltpu.VMEM((space, LANES), F32),
            pltpu.VMEM((space, LANES), F32),
            pltpu.VMEM((arch_count, 2 * LANES, LANES), BF16),
            pltpu.SMEM((8, LANES), jnp.int32),
            pltpu.SemaphoreType.DMA((6,)),
        ],
        compiler_params=params(),
    )(
        stay(live_counts),
        stay(archetype.reshape(1, rows_count)),
        stay(feeder.reshape(1, rows_count)),
        stay(load_base),
        stay(kkt_inverse),
        duals,
        cap,
    )
    gathered = lax.all_gather(sums, "dw", axis=0)
    pack, next_duals, rest = pl.pallas_call(
        lambda *refs: middle_kernel(steps, arch_count, *refs),
        name="middle",
        in_specs=[vmem()] * 2,
        out_specs=[vmem()] * 3,
        out_shape=[
            shape((arch_count + 8, LANES), F32),
            shape((feeders, LANES), F32),
            shape((feeders, 2 * LANES), F32),
        ],
        compiler_params=params(),
    )(gathered, duals)
    stride = 1
    other = jnp.zeros_like(pack)
    while stride < region_total:
        if stride > 1:
            pack = pack + other
        other = exchange(pack, "reg", stride)
        stride *= 2
    out, feeder_duals, balance_dual = pl.pallas_call(
        lambda *refs: last_kernel(inv_root, *refs),
        name="last",
        in_specs=[vmem()] * 10,
        out_specs=[hbm()] + [vmem()] * 2,
        out_shape=[
            shape((steps, rows_count), F32),
            shape((owned, steps), F32),
            shape((1, steps), F32),
        ],
        scratch_shapes=[
            pltpu.VMEM((space, LANES), F32),
            pltpu.VMEM((space, LANES), F32),
            pltpu.VMEM((space, 2 * LANES), BF16),
            pltpu.VMEM((EXTRA, LANES), F32),
            pltpu.VMEM((8, LANES), F32),
            pltpu.VMEM((steps, rows_count), F32),
            pltpu.SMEM((8, LANES), jnp.int32),
            pltpu.SemaphoreType.DMA,
            pltpu.SemaphoreType.DMA((rows_count // ROWS,)),
        ],
        compiler_params=params(),
    )(
        cap, offs, y, pos, next_duals, rest, pack, other, kkt_inverse,
        balance_target.reshape(1, steps),
    )
    return (out, feeder_duals, balance_dual.reshape(steps))


def solution(mesh):
    in_specs = (
        P(None, ("scen", "dw", "reg")),
        P(),
        P(("scen", "dw", "reg")),
        P(("scen", "dw", "reg")),
        P(("scen", "dw", "reg"), None),
        P(("scen", "dw", "reg")),
        P(("scen", "dw", "reg"), None),
        P("scen"),
    )
    out_specs = (P(None, ("scen", "dw", "reg")), P(("scen", "dw", "reg"), None), P("scen"))
    return jax.shard_map(
        on_device, mesh=mesh, in_specs=in_specs, out_specs=out_specs, check_vma=False
    )
```

```python
import math

import jax
import jax.numpy as jnp
from jax import lax
from jax.experimental import pallas as pl
from jax.experimental.pallas import tpu as pltpu
from jax.sharding import PartitionSpec as P

rho_weight = 0.5
dual_rate = 0.1
balance_rate = 1.0

LANES = 128
ROWS = 256
WIN = 48
BLOCKS = 8
EXTRA = 32
VMEM_BYTES = 24 * 1024 * 1024

F32 = jnp.float32
BF16 = jnp.bfloat16
NT = (((1,), (1,)), ((), ()))
TN = (((0,), (0,)), ((), ()))


def iota(shape, dim):
    return lax.broadcasted_iota(jnp.int32, shape, dim)


def halves(x):
    high = x.astype(BF16)
    return high, (x - high.astype(F32)).astype(BF16)


def side(x):
    return jnp.concatenate(halves(x), axis=1)


def mm(a, b, dims=None):
    if dims is None:
        return jnp.dot(a, b, preferred_element_type=F32)
    return lax.dot_general(a, b, dims, preferred_element_type=F32)


def fold(x):
    return x[:, :LANES] + x[:, LANES:]


def feeder_hot(rows, steps, count):
    label = jnp.broadcast_to(rows[:, steps : steps + 1], (rows.shape[0], count))
    lane = iota((rows.shape[0], count), 1).astype(F32)
    return jnp.where(label == lane + 1.0, 1.0, 0.0).astype(BF16)


def split_matrices(kkt_ref, mat_ref):
    arch_count, steps, _ = kkt_ref.shape
    for a in range(arch_count):
        high, low = halves(kkt_ref[a])
        mat_ref[a, 0:steps, 0:steps] = high
        mat_ref[a, LANES : LANES + steps, 0:steps] = low


def row_code(place):
    block = jnp.floor(place * (1.0 / ROWS))
    within = place - block * ROWS
    return jnp.where(within == iota((ROWS, place.shape[1]), 0).astype(F32), block, -1.0).astype(BF16)


def apply_matrix(x, matrix):
    count = x.shape[0]
    x = x[:, : matrix.shape[1]]
    rest = x - x.astype(BF16).astype(F32)
    both = mm(jnp.concatenate([x, rest], axis=0).astype(BF16), matrix, NT)
    return both[:count, :LANES] + (both[count:, :LANES] + both[:count, LANES:])


def each_group(offs_ref, arch_count, step):
    for a in range(arch_count):
        step(a, pl.multiple_of(offs_ref[0, a], 8), None)

    @pl.when(offs_ref[2, 0] > WIN)
    def _():
        def group(a, carry):
            start = offs_ref[0, a]
            size = (offs_ref[1, a] + 7) // 8 * 8

            def part(t, inner):
                step(a, pl.multiple_of(start + t * WIN, 8), size - t * WIN)
                return inner

            return lax.fori_loop(1, (size + WIN - 1) // WIN, part, carry)

        lax.fori_loop(0, arch_count, group, 0)


def tiers(most):
    return [t for t in (6, 7, 8) if t < most] + [most]


def put(ref, here, value, limit):
    if limit is not None:
        value = jnp.where(iota((WIN, LANES), 0) < limit, value, ref[here, :])
    ref[here, :] = value


def clear_after(offs_ref, refs):
    here = pl.ds(pl.multiple_of(offs_ref[3, 0], 8), WIN)
    for ref in refs:
        ref[here, :] = jnp.zeros((WIN, LANES), F32)


def each_block(blocks, step, total):
    for b in range(BLOCKS):
        total = step(b * ROWS, total)

    def more(b, inner):
        return step(pl.multiple_of(b * ROWS, ROWS), inner)

    return lax.fori_loop(BLOCKS, blocks, more, total)


def cap_column(cap_ref):
    owned = cap_ref.shape[1]
    cap = cap_ref[...].astype(F32) * 0.001
    diagonal = iota((owned, owned), 0) == iota((owned, owned), 1)
    return jnp.sum(jnp.where(diagonal, cap, 0.0), axis=1, keepdims=True)


def rank_kernel(
    owned, arch_count, counts_hbm, arch_hbm, feeder_hbm, pos_ref, label_ref, offs_ref, counts_ref, arch_ref, feeder_ref, sems
):
    copies = [
        pltpu.make_async_copy(a, b, sems.at[i])
        for i, (a, b) in enumerate([(counts_hbm, counts_ref), (arch_hbm, arch_ref), (feeder_hbm, feeder_ref)])
    ]
    for copy in copies:
        copy.start()
    rows_count = arch_ref.shape[1]
    block_total = counts_ref.shape[1]
    seg = rows_count // block_total
    for copy in copies:
        copy.wait()
    lane = iota((1, rows_count), 1)
    bound = jnp.zeros((1, rows_count), jnp.int32)
    base = jnp.zeros((1, rows_count), jnp.int32)
    for k in range(block_total):
        inside = lane >= k * seg
        bound = jnp.where(inside, k * seg + counts_ref[0, k], bound)
        base = jnp.where(inside, k * owned, base)
    live = lane < bound
    kind = jnp.where(live, arch_ref[...], -1)
    label_ref[...] = jnp.where(live, lax.rem(feeder_ref[...], owned) + base + 1, 0).astype(F32)

    chunk = 256
    before = jnp.where(iota((chunk, chunk), 0) < iota((chunk, chunk), 1), 1.0, 0.0).astype(BF16)
    arch_iota = iota((arch_count, chunk), 0)
    carry = jnp.zeros((arch_count, 1), F32)
    hots, ranks = [], []
    for c in range(rows_count // chunk):
        hot = jnp.where(kind[:, c * chunk : (c + 1) * chunk] == arch_iota, 1.0, 0.0)
        ranks.append(mm(hot.astype(BF16), before) + carry)
        hots.append(hot)
        carry = carry + jnp.sum(hot, axis=1, keepdims=True)
    eights = jnp.floor((carry + 7.0) * 0.125)
    lower = jnp.where(iota((arch_count, arch_count), 1) < iota((arch_count, arch_count), 0), 1.0, 0.0).astype(BF16)
    offs = mm(lower, jnp.broadcast_to(eights, (arch_count, LANES)).astype(BF16)) * 8.0
    for c in range(rows_count // chunk):
        part = slice(c * chunk, (c + 1) * chunk)
        place = jnp.sum(hots[c] * (ranks[c] + offs[:, :1]), axis=0, keepdims=True)
        place = jnp.where(live[:, part], place, -1.0)
        pos_ref[:, part] = place.astype(jnp.int32)
    diagonal = iota((arch_count, LANES), 0) == iota((arch_count, LANES), 1)
    offs_row = jnp.sum(jnp.where(diagonal, offs, 0.0), axis=0, keepdims=True)
    size_row = jnp.sum(jnp.where(diagonal, jnp.broadcast_to(carry, (arch_count, LANES)), 0.0), axis=0, keepdims=True)
    used = (jnp.sum(eights) * 8.0).astype(jnp.int32)
    blocks = (used + ROWS - 1) // ROWS
    row = iota((8, LANES), 0)
    table = jnp.where(row == 0, offs_row, jnp.where(row == 1, size_row, 0.0)).astype(jnp.int32)
    biggest = jnp.max(carry).astype(jnp.int32)
    offs_ref[...] = jnp.where(row == 2, biggest, jnp.where(row == 3, used, jnp.where(row == 4, blocks, table)))


def first_kernel(block_total, load_hbm, kkt_hbm, start_hbm, cap_hbm, pos_ref, label_ref, offs_vmem, *rest):
    piece_refs = rest[:-15]
    y_ref, sums_ref, duals_ref, load_ref, kkt_ref, start_ref, cap_ref, xt_ref, code_ref, xs_ref, z_ref, r_ref, mat_ref, offs_ref, sems = rest[-15:]
    copies = [
        pltpu.make_async_copy(a, b, sems.at[i])
        for i, (a, b) in enumerate([
                (load_hbm, load_ref),
                (kkt_hbm, kkt_ref),
                (offs_vmem, offs_ref),
                (start_hbm, start_ref),
                (cap_hbm, cap_ref),
            ])
    ]
    for copy in copies:
        copy.start()
    arch_count, steps, _ = kkt_ref.shape
    rows_count = load_ref.shape[1]
    feeders = duals_ref.shape[0]
    owned = feeders // block_total
    own = lax.axis_index("dw")
    spare = LANES - steps
    label = label_ref[...]
    blocks = jnp.max(offs_vmem[4:5, :])
    mat_ref[...] = jnp.zeros_like(mat_ref)
    for c in range(rows_count // ROWS):
        part = slice(c * ROWS, (c + 1) * ROWS)
        code_ref[:, part] = row_code(pos_ref[:, part].astype(F32))

    copies[3].wait()
    copies[4].wait()
    duals_ref[...] = jnp.zeros_like(duals_ref)
    if len(piece_refs) == 1:
        duals_ref[:, 0:steps] = piece_refs[0][...]
    else:
        for p, ref in enumerate([start_ref, *piece_refs]):
            duals_ref[pl.ds(pl.multiple_of((own ^ p) * owned, owned), owned), 0:steps] = ref[...]
    duals_side = side(duals_ref[...])
    copies[0].wait()
    for c in range(rows_count // LANES):
        part = slice(c * LANES, (c + 1) * LANES)
        extra = jnp.where(iota((LANES - steps, LANES), 0) == 0, label[:, part], 0.0)
        block = jnp.concatenate([load_ref[:, part], extra], axis=0).T
        xt_ref[part, :] = side(block)

    copies[1].wait()
    split_matrices(kkt_ref, mat_ref)

    def permute(b, inner):
        at = pl.multiple_of(b * ROWS, ROWS)
        hot = jnp.where(code_ref[...] == b.astype(F32).astype(BF16), 1.0, 0.0).astype(BF16)
        xs_ref[pl.ds(at, ROWS), :] = fold(mm(hot, xt_ref[...]))
        return inner

    lax.fori_loop(0, blocks, permute, 0)

    def pick(at, inner):
        here = pl.ds(at, ROWS)
        xs = xs_ref[here, :]
        z_ref[here, :] = xs - fold(mm(feeder_hot(xs, steps, feeders), duals_side))
        r_ref[here, :] = jnp.zeros((ROWS, LANES), F32)
        y_ref[here, :] = jnp.zeros((ROWS, LANES), F32)
        return inner

    each_block(blocks, pick, 0)
    copies[2].wait()

    is_label = iota((WIN, LANES), 1) == steps

    def group(a, row, limit):
        here = pl.ds(row, WIN)
        xs = xs_ref[here, :]
        matrix = mat_ref[a]
        r = apply_matrix(z_ref[here, :], matrix)
        put(r_ref, here, r, limit)
        y = apply_matrix(xs + rho_weight * r, matrix)
        put(y_ref, here, jnp.where(is_label, xs, y), limit)

    each_group(offs_ref, arch_count, group)
    clear_after(offs_ref, [r_ref, y_ref])

    offs_row = offs_vmem[0:1, :]
    ends_row = offs_row + offs_vmem[1:2, :]

    def gather(at, total):
        here = pl.ds(at, ROWS)
        row = iota((ROWS, LANES), 0) + at
        member = jnp.where((row >= offs_row) & (row < ends_row), 1.0, 0.0).astype(BF16)
        y = y_ref[here, :]
        right = jnp.concatenate([*halves(r_ref[here, :]), *halves(y), member], axis=1)
        return total + mm(feeder_hot(y, steps, feeders), right, TN)

    sums = each_block(blocks, gather, jnp.zeros((feeders, 5 * LANES), F32))
    loads = sums[:, 0:LANES] + sums[:, LANES : 2 * LANES]
    others = sums[:, 2 * LANES : 3 * LANES] + sums[:, 3 * LANES : 4 * LANES]
    counts = sums[:, 4 * LANES :]
    low = jnp.concatenate([counts[:, spare : spare + steps], counts[:, 0:spare]], axis=1)
    high = jnp.concatenate([counts[:, 2 * spare : LANES], counts[:, 0 : 2 * spare]], axis=1)
    lane = iota((feeders, LANES), 1)
    sums_ref[0:feeders, 0:LANES] = jnp.where(lane < steps, loads, low)
    sums_ref[0:feeders, LANES:] = jnp.where(lane < steps, others, high)
    row = iota((8, LANES), 0)
    sums_ref[feeders:, 0:LANES] = jnp.where(row == 0, jnp.sum(loads, axis=0, keepdims=True), 0.0)
    sums_ref[feeders:, LANES:] = jnp.where(row == 0, jnp.sum(others, axis=0, keepdims=True), 0.0)
    mine = pl.ds(pl.multiple_of(own * owned, owned), owned)
    cap = jnp.where(iota((owned, LANES), 1) < steps, cap_column(cap_ref), 0.0)
    sums_ref[mine, 0:LANES] = sums_ref[mine, 0:LANES] - cap


def middle_kernel(steps, arch_count, sums_ref, duals_ref, pack_ref, next_ref, rest_ref):
    total = sums_ref[0]
    for d in range(1, sums_ref.shape[0]):
        total = total + sums_ref[d]
    feeders = duals_ref.shape[0]
    spare = LANES - steps
    excess = total[:feeders, :LANES]
    others = total[:feeders, LANES:]
    lane = iota((feeders, LANES), 1)
    after = jnp.maximum(duals_ref[...] + dual_rate * excess, 0.0)
    after = jnp.where(lane < steps, after, jnp.where(lane == steps, 1.0, 0.0))
    next_ref[...] = after
    counts = jnp.concatenate([excess[:, steps:], others[:, steps:], jnp.zeros((feeders, LANES - 2 * spare), F32)], axis=1)
    rest_ref[:, :LANES] = others
    rest_ref[:, LANES:] = counts
    mixed = lax.dot_general(counts, after, TN, precision=lax.Precision.HIGHEST, preferred_element_type=F32)
    pack_ref[0:arch_count, :] = mixed[:arch_count]
    row = iota((8, LANES), 0)
    pack_ref[arch_count:, :] = jnp.where(
        row == 0, total[feeders : feeders + 1, :LANES], jnp.where(row == 1, total[feeders : feeders + 1, LANES:], 0.0)
    )


def last_kernel(
    inv_root, cap_ref, offs_vmem, y_ref, pos_ref, duals_ref, rest_ref, left_ref, right_ref, kkt_ref, target_ref,
    out_hbm, feeder_ref, balance_ref,
    z_ref, r_ref, side_ref, mat_ref, code_ref, acc_ref, target_pad, stage_ref, offs_ref, sem, out_sems,
):
    copy = pltpu.make_async_copy(offs_vmem, offs_ref, sem)
    copy.start()
    arch_count = kkt_ref.shape[0]
    owned = cap_ref.shape[1]
    steps = target_ref.shape[1]
    rows_count = pos_ref.shape[1]
    feeders = duals_ref.shape[0]
    pack = left_ref[...] + right_ref[...]
    target_pad[...] = jnp.zeros_like(target_pad)
    target_pad[0:1, 0:steps] = target_ref[...]
    target = target_pad[0:1, :]
    balance = balance_rate * (pack[arch_count : arch_count + 1] * inv_root - target)
    mixed = pack[:arch_count]
    mixed = mixed + mixed[:, steps : steps + 1] * balance
    duals_all = duals_ref[...] + balance
    duals_side = side(duals_all)
    own = pl.ds(pl.multiple_of(lax.axis_index("dw") * owned, owned), owned)
    own_before = duals_ref[own, :]
    own_duals = own_before + balance
    own_rest = rest_ref[own, :]
    blocks = jnp.max(offs_vmem[4:5, :])

    def pick(at, inner):
        here = pl.ds(at, ROWS)
        z_ref[here, :] = fold(mm(feeder_hot(y_ref[here, :], steps, feeders), duals_side))
        r_ref[here, :] = jnp.zeros((ROWS, LANES), F32)
        return inner

    each_block(blocks, pick, 0)
    mat_ref[...] = jnp.zeros_like(mat_ref)
    split_matrices(kkt_ref, mat_ref)
    for c in range(rows_count // ROWS):
        part = slice(c * ROWS, (c + 1) * ROWS)
        code_ref[:, part] = row_code(pos_ref[:, part].astype(F32))
    copy.wait()

    first = iota((EXTRA - owned, LANES), 0) == 0
    acc_ref[...] = jnp.zeros_like(acc_ref)

    def group(a, row, limit):
        here = pl.ds(row, WIN)
        matrix = mat_ref[a]
        if limit is not None:
            put(r_ref, here, y_ref[here, :] - apply_matrix(z_ref[here, :], matrix), limit)
            return
        rows = own_rest[:, LANES + a : LANES + a + 1] * own_duals
        more = jnp.where(first, mixed[a : a + 1], 0.0)
        done = apply_matrix(jnp.concatenate([z_ref[here, :], rows, more], axis=0), matrix)
        r_ref[here, :] = y_ref[here, :] - done[:WIN]
        acc_ref[...] += done[WIN:]

    each_group(offs_ref, arch_count, group)
    clear_after(offs_ref, [r_ref])
    acc = acc_ref[...]

    loads = own_rest[:, :LANES] - acc[:owned]
    after = jnp.maximum(own_before + dual_rate * (loads - cap_column(cap_ref)), 0.0)
    feeder_ref[...] = after[:, :steps]
    system = pack[arch_count + 1 : arch_count + 2] - acc[owned : owned + 1]
    balance_ref[...] = (balance + balance_rate * (system * inv_root - target))[:, :steps]

    def columns(c, reach):
        part = pl.ds(pl.multiple_of(c * ROWS, ROWS), ROWS)
        code = code_ref[:, part]
        hot = jnp.concatenate([jnp.where(code == jnp.bfloat16(q), 1.0, 0.0).astype(BF16) for q in range(reach)], axis=0)
        both = mm(side_ref[:, 0 : reach * ROWS], hot)
        stage_ref[:, part] = both[:steps] + both[steps:]
        return pltpu.make_async_copy(stage_ref.at[:, part], out_hbm.at[:, part], out_sems.at[c])

    def spread(reach):
        def pair(c, inner):
            for half in range(2):
                columns(2 * c + half, reach).start()
            return inner

        lax.fori_loop(0, rows_count // (2 * ROWS), pair, 0)

    count = blocks
    low = 0
    for reach in tiers(y_ref.shape[0] // ROWS):
        @pl.when((count > low) & (count <= reach))
        def _():
            for b in range(reach):
                here = slice(b * ROWS, (b + 1) * ROWS)
                turned = r_ref[here, :].T[:steps]
                side_ref[:, here] = jnp.concatenate(halves(turned), axis=0)
            spread(reach)

        low = reach

    for c in range(rows_count // ROWS):
        part = slice(c * ROWS, (c + 1) * ROWS)
        pltpu.make_async_copy(stage_ref.at[:, part], out_hbm.at[:, part], out_sems.at[c]).wait()


def vmem():
    return pl.BlockSpec(memory_space=pltpu.VMEM)


def hbm():
    return pl.BlockSpec(memory_space=pltpu.HBM)


def stay(x):
    return pltpu.with_memory_space_constraint(x, pltpu.HBM)


def params():
    return pltpu.CompilerParams(vmem_limit_bytes=VMEM_BYTES)


def exchange(x, axis, mask):
    return lax.ppermute(x, axis, [(i, i ^ mask) for i in range(lax.axis_size(axis))])


def on_device(
    load_base, kkt_inverse, archetype, feeder, live_counts, feeder_cap, dual_start, balance_target
):
    steps, rows_count = load_base.shape
    arch_count = kkt_inverse.shape[0]
    block_total = lax.axis_size("dw")
    region_total = lax.axis_size("reg")
    owned = dual_start.shape[0]
    feeders = owned * block_total
    inv_root = 1.0 / math.sqrt(rows_count * block_total * region_total)
    space = -(-(rows_count + 7 * arch_count + ROWS + WIN) // ROWS) * ROWS
    shape = jax.ShapeDtypeStruct
    cap = feeder_cap.reshape(1, owned)
    paired = block_total == 4
    if paired:
        far = exchange(dual_start, "dw", 2)
    pos, label, offs = pl.pallas_call(
        lambda *refs: rank_kernel(owned, arch_count, *refs),
        name="rank",
        in_specs=[hbm()] * 3,
        out_specs=[vmem()] * 3,
        out_shape=[
            shape((1, rows_count), jnp.int32),
            shape((1, rows_count), F32),
            shape((8, LANES), jnp.int32),
        ],
        scratch_shapes=[
            pltpu.SMEM((1, block_total), jnp.int32),
            pltpu.VMEM((1, rows_count), jnp.int32),
            pltpu.VMEM((1, rows_count), jnp.int32),
            pltpu.SemaphoreType.DMA((3,)),
        ],
        compiler_params=params(),
    )(stay(live_counts), stay(archetype.reshape(1, rows_count)), stay(feeder.reshape(1, rows_count)))
    if paired:
        far, offs = lax.optimization_barrier((far, offs))
        pieces = [exchange(dual_start, "dw", 1), far, exchange(far, "dw", 1)]
    else:
        pieces = [lax.all_gather(dual_start, "dw", axis=0, tiled=True)]
    y, sums, duals = pl.pallas_call(
        lambda *refs: first_kernel(block_total, *refs),
        name="first",
        in_specs=[hbm()] * 4 + [vmem()] * (3 + len(pieces)),
        out_specs=[vmem()] * 3,
        out_shape=[
            shape((space, LANES), F32),
            shape((feeders + 8, 2 * LANES), F32),
            shape((feeders, LANES), F32),
        ],
        scratch_shapes=[
            pltpu.VMEM((steps, rows_count), F32),
            pltpu.VMEM((arch_count, steps, steps), F32),
            pltpu.VMEM((owned, steps), F32),
            pltpu.VMEM((1, owned), jnp.int32),
            pltpu.VMEM((rows_count, 2 * LANES), BF16),
            pltpu.VMEM((ROWS, rows_count), BF16),
            pltpu.VMEM((space, LANES), F32),
            pltpu.VMEM((space, LANES), F32),
            pltpu.VMEM((space, LANES), F32),
            pltpu.VMEM((arch_count, 2 * LANES, LANES), BF16),
            pltpu.SMEM((8, LANES), jnp.int32),
            pltpu.SemaphoreType.DMA((5,)),
        ],
        compiler_params=params(),
    )(stay(load_base), stay(kkt_inverse), stay(dual_start), stay(cap), pos, label, offs, *pieces)
    gathered = lax.all_gather(sums, "dw", axis=0)
    pack, next_duals, rest = pl.pallas_call(
        lambda *refs: middle_kernel(steps, arch_count, *refs),
        name="middle",
        in_specs=[vmem()] * 2,
        out_specs=[vmem()] * 3,
        out_shape=[
            shape((arch_count + 8, LANES), F32),
            shape((feeders, LANES), F32),
            shape((feeders, 2 * LANES), F32),
        ],
        compiler_params=params(),
    )(gathered, duals)
    stride = 1
    other = jnp.zeros_like(pack)
    while stride < region_total:
        if stride > 1:
            pack = pack + other
        other = exchange(pack, "reg", stride)
        stride *= 2
    out, feeder_duals, balance_dual = pl.pallas_call(
        lambda *refs: last_kernel(inv_root, *refs),
        name="last",
        in_specs=[vmem()] * 10,
        out_specs=[hbm()] + [vmem()] * 2,
        out_shape=[
            shape((steps, rows_count), F32),
            shape((owned, steps), F32),
            shape((1, steps), F32),
        ],
        scratch_shapes=[
            pltpu.VMEM((space, LANES), F32),
            pltpu.VMEM((space, LANES), F32),
            pltpu.VMEM((2 * steps, space), BF16),
            pltpu.VMEM((arch_count, 2 * LANES, LANES), BF16),
            pltpu.VMEM((ROWS, rows_count), BF16),
            pltpu.VMEM((EXTRA, LANES), F32),
            pltpu.VMEM((8, LANES), F32),
            pltpu.VMEM((steps, rows_count), F32),
            pltpu.SMEM((8, LANES), jnp.int32),
            pltpu.SemaphoreType.DMA,
            pltpu.SemaphoreType.DMA((rows_count // ROWS,)),
        ],
        compiler_params=params(),
    )(
        cap, offs, y, pos, next_duals, rest, pack, other, kkt_inverse,
        balance_target.reshape(1, steps),
    )
    return (out, feeder_duals, balance_dual.reshape(steps))


def solution(mesh):
    in_specs = (
        P(None, ("scen", "dw", "reg")),
        P(),
        P(("scen", "dw", "reg")),
        P(("scen", "dw", "reg")),
        P(("scen", "dw", "reg"), None),
        P(("scen", "dw", "reg")),
        P(("scen", "dw", "reg"), None),
        P("scen"),
    )
    out_specs = (P(None, ("scen", "dw", "reg")), P(("scen", "dw", "reg"), None), P("scen"))
    return jax.shard_map(
        on_device, mesh=mesh, in_specs=in_specs, out_specs=out_specs, check_vma=False
    )
```

```python
import math

import jax
import jax.numpy as jnp
from jax import lax
from jax.experimental import pallas as pl
from jax.experimental.pallas import tpu as pltpu
from jax.sharding import PartitionSpec as P

rho_weight = 0.5
dual_rate = 0.1
balance_rate = 1.0

LANES = 128
ROWS = 256
WIN = 48
BLOCKS = 8
EXTRA = 24
VMEM_BYTES = 24 * 1024 * 1024

F32 = jnp.float32
BF16 = jnp.bfloat16
NT = (((1,), (1,)), ((), ()))
TN = (((0,), (0,)), ((), ()))


def iota(shape, dim):
    return lax.broadcasted_iota(jnp.int32, shape, dim)


def halves(x):
    high = x.astype(BF16)
    return high, (x - high.astype(F32)).astype(BF16)


def side(x):
    return jnp.concatenate(halves(x), axis=1)


def mm(a, b, dims=None):
    if dims is None:
        return jnp.dot(a, b, preferred_element_type=F32)
    return lax.dot_general(a, b, dims, preferred_element_type=F32)


def fold(x):
    return x[:, :LANES] + x[:, LANES:]


def feeder_hot(rows, steps, count):
    label = jnp.broadcast_to(rows[:, steps : steps + 1], (rows.shape[0], count))
    lane = iota((rows.shape[0], count), 1).astype(F32)
    return jnp.where(label == lane + 1.0, 1.0, 0.0).astype(BF16)


def split_matrices(kkt_ref, mat_ref):
    arch_count, steps, _ = kkt_ref.shape
    for a in range(arch_count):
        high, low = halves(kkt_ref[a].T)
        mat_ref[a, 0:steps, 0:steps] = high
        mat_ref[a, 0:steps, LANES : LANES + steps] = low


def row_code(place):
    block = jnp.floor(place * (1.0 / ROWS))
    within = place - block * ROWS
    return jnp.where(within == iota((ROWS, place.shape[1]), 0).astype(F32), block, -1.0).astype(BF16)


def apply_matrix(x, matrix):
    count = x.shape[0]
    rest = x - x.astype(BF16).astype(F32)
    both = mm(jnp.concatenate([x, rest], axis=0).astype(BF16), matrix)
    return both[:count, :LANES] + (both[count:, :LANES] + both[:count, LANES:])


def each_group(offs_ref, arch_count, step):
    for a in range(arch_count):
        step(a, pl.multiple_of(offs_ref[0, a], 8), None)

    @pl.when(offs_ref[2, 0] > WIN)
    def _():
        def group(a, carry):
            start = offs_ref[0, a]
            size = (offs_ref[1, a] + 7) // 8 * 8

            def part(t, inner):
                step(a, pl.multiple_of(start + t * WIN, 8), size - t * WIN)
                return inner

            return lax.fori_loop(1, (size + WIN - 1) // WIN, part, carry)

        lax.fori_loop(0, arch_count, group, 0)


def tiers(most):
    return [t for t in (6, 7, 8) if t < most] + [most]


def put(ref, here, value, limit):
    if limit is not None:
        value = jnp.where(iota((WIN, LANES), 0) < limit, value, ref[here, :])
    ref[here, :] = value


def clear_after(offs_ref, refs):
    here = pl.ds(pl.multiple_of(offs_ref[3, 0], 8), WIN)
    for ref in refs:
        ref[here, :] = jnp.zeros((WIN, LANES), F32)


def each_block(blocks, step, total):
    for b in range(BLOCKS):
        total = step(b * ROWS, total)

    def more(b, inner):
        return step(pl.multiple_of(b * ROWS, ROWS), inner)

    return lax.fori_loop(BLOCKS, blocks, more, total)


def cap_column(cap_ref):
    owned = cap_ref.shape[1]
    cap = cap_ref[...].astype(F32) * 0.001
    diagonal = iota((owned, owned), 0) == iota((owned, owned), 1)
    return jnp.sum(jnp.where(diagonal, cap, 0.0), axis=1, keepdims=True)


def rank_kernel(
    owned, arch_count, counts_hbm, arch_hbm, feeder_hbm, pos_ref, label_ref, offs_ref, counts_ref, arch_ref, feeder_ref, sems
):
    copies = [
        pltpu.make_async_copy(a, b, sems.at[i])
        for i, (a, b) in enumerate([(counts_hbm, counts_ref), (arch_hbm, arch_ref), (feeder_hbm, feeder_ref)])
    ]
    for copy in copies:
        copy.start()
    rows_count = arch_ref.shape[1]
    block_total = counts_ref.shape[1]
    seg = rows_count // block_total
    for copy in copies:
        copy.wait()
    lane = iota((1, rows_count), 1)
    bound = jnp.zeros((1, rows_count), jnp.int32)
    base = jnp.zeros((1, rows_count), jnp.int32)
    for k in range(block_total):
        inside = lane >= k * seg
        bound = jnp.where(inside, k * seg + counts_ref[0, k], bound)
        base = jnp.where(inside, k * owned, base)
    live = lane < bound
    kind = jnp.where(live, arch_ref[...], -1)
    label_ref[...] = jnp.where(live, lax.rem(feeder_ref[...], owned) + base + 1, 0).astype(F32)

    chunk = 256
    before = jnp.where(iota((chunk, chunk), 0) < iota((chunk, chunk), 1), 1.0, 0.0).astype(BF16)
    arch_iota = iota((arch_count, chunk), 0)
    carry = jnp.zeros((arch_count, 1), F32)
    hots, ranks = [], []
    for c in range(rows_count // chunk):
        hot = jnp.where(kind[:, c * chunk : (c + 1) * chunk] == arch_iota, 1.0, 0.0)
        ranks.append(mm(hot.astype(BF16), before) + carry)
        hots.append(hot)
        carry = carry + jnp.sum(hot, axis=1, keepdims=True)
    eights = jnp.floor((carry + 7.0) * 0.125)
    lower = jnp.where(iota((arch_count, arch_count), 1) < iota((arch_count, arch_count), 0), 1.0, 0.0).astype(BF16)
    offs = mm(lower, jnp.broadcast_to(eights, (arch_count, LANES)).astype(BF16)) * 8.0
    for c in range(rows_count // chunk):
        part = slice(c * chunk, (c + 1) * chunk)
        place = jnp.sum(hots[c] * (ranks[c] + offs[:, :1]), axis=0, keepdims=True)
        place = jnp.where(live[:, part], place, -1.0)
        pos_ref[:, part] = place.astype(jnp.int32)
    diagonal = iota((arch_count, LANES), 0) == iota((arch_count, LANES), 1)
    offs_row = jnp.sum(jnp.where(diagonal, offs, 0.0), axis=0, keepdims=True)
    size_row = jnp.sum(jnp.where(diagonal, jnp.broadcast_to(carry, (arch_count, LANES)), 0.0), axis=0, keepdims=True)
    used = (jnp.sum(eights) * 8.0).astype(jnp.int32)
    blocks = (used + ROWS - 1) // ROWS
    row = iota((8, LANES), 0)
    table = jnp.where(row == 0, offs_row, jnp.where(row == 1, size_row, 0.0)).astype(jnp.int32)
    biggest = jnp.max(carry).astype(jnp.int32)
    offs_ref[...] = jnp.where(row == 2, biggest, jnp.where(row == 3, used, jnp.where(row == 4, blocks, table)))


def first_kernel(block_total, load_hbm, kkt_hbm, start_hbm, cap_hbm, pos_ref, label_ref, offs_vmem, *rest):
    piece_refs = rest[:-15]
    y_ref, sums_ref, duals_ref, load_ref, kkt_ref, start_ref, cap_ref, xt_ref, code_ref, xs_ref, z_ref, r_ref, mat_ref, offs_ref, sems = rest[-15:]
    copies = [
        pltpu.make_async_copy(a, b, sems.at[i])
        for i, (a, b) in enumerate([
                (load_hbm, load_ref),
                (kkt_hbm, kkt_ref),
                (offs_vmem, offs_ref),
                (start_hbm, start_ref),
                (cap_hbm, cap_ref),
            ])
    ]
    for copy in copies:
        copy.start()
    arch_count, steps, _ = kkt_ref.shape
    rows_count = load_ref.shape[1]
    feeders = duals_ref.shape[0]
    owned = feeders // block_total
    own = lax.axis_index("dw")
    spare = LANES - steps
    label = label_ref[...]
    blocks = jnp.max(offs_vmem[4:5, :])
    mat_ref[...] = jnp.zeros_like(mat_ref)
    for c in range(rows_count // ROWS):
        part = slice(c * ROWS, (c + 1) * ROWS)
        code_ref[:, part] = row_code(pos_ref[:, part].astype(F32))

    copies[3].wait()
    copies[4].wait()
    duals_ref[...] = jnp.zeros_like(duals_ref)
    if len(piece_refs) == 1:
        duals_ref[:, 0:steps] = piece_refs[0][...]
    else:
        for p, ref in enumerate([start_ref, *piece_refs]):
            duals_ref[pl.ds(pl.multiple_of((own ^ p) * owned, owned), owned), 0:steps] = ref[...]
    duals_side = side(duals_ref[...])
    copies[0].wait()
    for c in range(rows_count // LANES):
        part = slice(c * LANES, (c + 1) * LANES)
        extra = jnp.where(iota((LANES - steps, LANES), 0) == 0, label[:, part], 0.0)
        block = jnp.concatenate([load_ref[:, part], extra], axis=0).T
        xt_ref[part, :] = side(block)

    copies[1].wait()
    split_matrices(kkt_ref, mat_ref)

    def permute(at, inner):
        number = jnp.asarray(at // ROWS, jnp.int32).astype(F32).astype(BF16)
        hot = jnp.where(code_ref[...] == number, 1.0, 0.0).astype(BF16)
        xs_ref[pl.ds(at, ROWS), :] = fold(mm(hot, xt_ref[...]))
        return inner

    each_block(blocks, permute, 0)

    def pick(at, inner):
        here = pl.ds(at, ROWS)
        xs = xs_ref[here, :]
        z_ref[here, :] = xs - fold(mm(feeder_hot(xs, steps, feeders), duals_side))
        r_ref[here, :] = jnp.zeros((ROWS, LANES), F32)
        y_ref[here, :] = jnp.zeros((ROWS, LANES), F32)
        return inner

    each_block(blocks, pick, 0)
    copies[2].wait()

    is_label = iota((WIN, LANES), 1) == steps

    def group(a, row, limit):
        here = pl.ds(row, WIN)
        xs = xs_ref[here, :]
        matrix = mat_ref[a]
        r = apply_matrix(z_ref[here, :], matrix)
        put(r_ref, here, r, limit)
        y = apply_matrix(xs + rho_weight * r, matrix)
        put(y_ref, here, jnp.where(is_label, xs, y), limit)

    each_group(offs_ref, arch_count, group)
    clear_after(offs_ref, [r_ref, y_ref])

    offs_row = offs_vmem[0:1, :]
    ends_row = offs_row + offs_vmem[1:2, :]

    def gather(at, total):
        here = pl.ds(at, ROWS)
        row = iota((ROWS, LANES), 0) + at
        member = jnp.where((row >= offs_row) & (row < ends_row), 1.0, 0.0).astype(BF16)
        y = y_ref[here, :]
        right = jnp.concatenate([*halves(r_ref[here, :]), *halves(y), member], axis=1)
        return total + mm(feeder_hot(y, steps, feeders), right, TN)

    sums = each_block(blocks, gather, jnp.zeros((feeders, 5 * LANES), F32))
    loads = sums[:, 0:LANES] + sums[:, LANES : 2 * LANES]
    others = sums[:, 2 * LANES : 3 * LANES] + sums[:, 3 * LANES : 4 * LANES]
    counts = sums[:, 4 * LANES :]
    low = jnp.concatenate([counts[:, spare : spare + steps], counts[:, 0:spare]], axis=1)
    high = jnp.concatenate([counts[:, 2 * spare : LANES], counts[:, 0 : 2 * spare]], axis=1)
    lane = iota((feeders, LANES), 1)
    sums_ref[0:feeders, 0:LANES] = jnp.where(lane < steps, loads, low)
    sums_ref[0:feeders, LANES:] = jnp.where(lane < steps, others, high)
    row = iota((8, LANES), 0)
    sums_ref[feeders:, 0:LANES] = jnp.where(row == 0, jnp.sum(loads, axis=0, keepdims=True), 0.0)
    sums_ref[feeders:, LANES:] = jnp.where(row == 0, jnp.sum(others, axis=0, keepdims=True), 0.0)
    mine = pl.ds(pl.multiple_of(own * owned, owned), owned)
    cap = jnp.where(iota((owned, LANES), 1) < steps, cap_column(cap_ref), 0.0)
    sums_ref[mine, 0:LANES] = sums_ref[mine, 0:LANES] - cap


def middle_kernel(steps, arch_count, sums_ref, duals_ref, pack_ref, next_ref, rest_ref):
    total = sums_ref[0]
    for d in range(1, sums_ref.shape[0]):
        total = total + sums_ref[d]
    feeders = duals_ref.shape[0]
    spare = LANES - steps
    excess = total[:feeders, :LANES]
    others = total[:feeders, LANES:]
    lane = iota((feeders, LANES), 1)
    after = jnp.maximum(duals_ref[...] + dual_rate * excess, 0.0)
    after = jnp.where(lane < steps, after, jnp.where(lane == steps, 1.0, 0.0))
    next_ref[...] = after
    counts = jnp.concatenate([excess[:, steps:], others[:, steps:], jnp.zeros((feeders, LANES - 2 * spare), F32)], axis=1)
    rest_ref[:, :LANES] = others
    rest_ref[:, LANES:] = counts
    mixed = lax.dot_general(counts, after, TN, precision=lax.Precision.HIGHEST, preferred_element_type=F32)
    pack_ref[0:arch_count, :] = mixed[:arch_count]
    row = iota((8, LANES), 0)
    pack_ref[arch_count:, :] = jnp.where(
        row == 0, total[feeders : feeders + 1, :LANES], jnp.where(row == 1, total[feeders : feeders + 1, LANES:], 0.0)
    )


def last_kernel(
    inv_root, cap_ref, offs_vmem, y_ref, pos_ref, duals_ref, rest_ref, left_ref, right_ref, kkt_ref, target_ref,
    out_hbm, feeder_ref, balance_ref,
    z_ref, r_ref, side_ref, mat_ref, code_ref, acc_ref, target_pad, stage_ref, offs_ref, sem, out_sems,
):
    copy = pltpu.make_async_copy(offs_vmem, offs_ref, sem)
    copy.start()
    arch_count = kkt_ref.shape[0]
    owned = cap_ref.shape[1]
    steps = target_ref.shape[1]
    rows_count = pos_ref.shape[1]
    feeders = duals_ref.shape[0]
    pack = left_ref[...] + right_ref[...]
    target_pad[...] = jnp.zeros_like(target_pad)
    target_pad[0:1, 0:steps] = target_ref[...]
    target = target_pad[0:1, :]
    balance = balance_rate * (pack[arch_count : arch_count + 1] * inv_root - target)
    mixed = pack[:arch_count]
    mixed = mixed + mixed[:, steps : steps + 1] * balance
    duals_all = duals_ref[...] + balance
    duals_side = side(duals_all)
    own = pl.ds(pl.multiple_of(lax.axis_index("dw") * owned, owned), owned)
    own_before = duals_ref[own, :]
    own_duals = own_before + balance
    own_rest = rest_ref[own, :]
    blocks = jnp.max(offs_vmem[4:5, :])

    def pick(at, inner):
        here = pl.ds(at, ROWS)
        z_ref[here, :] = fold(mm(feeder_hot(y_ref[here, :], steps, feeders), duals_side))
        r_ref[here, :] = jnp.zeros((ROWS, LANES), F32)
        return inner

    each_block(blocks, pick, 0)
    mat_ref[...] = jnp.zeros_like(mat_ref)
    split_matrices(kkt_ref, mat_ref)
    for c in range(rows_count // ROWS):
        part = slice(c * ROWS, (c + 1) * ROWS)
        code_ref[:, part] = row_code(pos_ref[:, part].astype(F32))
    copy.wait()

    first = iota((EXTRA - owned, LANES), 0) == 0
    acc_ref[...] = jnp.zeros_like(acc_ref)

    def group(a, row, limit):
        here = pl.ds(row, WIN)
        matrix = mat_ref[a]
        if limit is not None:
            put(r_ref, here, y_ref[here, :] - apply_matrix(z_ref[here, :], matrix), limit)
            return
        rows = own_rest[:, LANES + a : LANES + a + 1] * own_duals
        more = jnp.where(first, mixed[a : a + 1], 0.0)
        done = apply_matrix(jnp.concatenate([z_ref[here, :], rows, more], axis=0), matrix)
        r_ref[here, :] = y_ref[here, :] - done[:WIN]
        acc_ref[...] += done[WIN:]

    each_group(offs_ref, arch_count, group)
    clear_after(offs_ref, [r_ref])
    acc = acc_ref[...]

    loads = own_rest[:, :LANES] - acc[:owned]
    after = jnp.maximum(own_before + dual_rate * (loads - cap_column(cap_ref)), 0.0)
    feeder_ref[...] = after[:, :steps]
    system = pack[arch_count + 1 : arch_count + 2] - acc[owned : owned + 1]
    balance_ref[...] = (balance + balance_rate * (system * inv_root - target))[:, :steps]

    def columns(c, reach):
        part = pl.ds(pl.multiple_of(c * ROWS, ROWS), ROWS)
        code = code_ref[:, part]
        hot = jnp.concatenate([jnp.where(code == jnp.bfloat16(q), 1.0, 0.0).astype(BF16) for q in range(reach)], axis=0)
        both = mm(side_ref[:, 0 : reach * ROWS], hot)
        stage_ref[:, part] = both[:steps] + both[steps:]
        return pltpu.make_async_copy(stage_ref.at[:, part], out_hbm.at[:, part], out_sems.at[c])

    def spread(reach):
        def pair(c, inner):
            for part in range(4):
                columns(4 * c + part, reach).start()
            return inner

        lax.fori_loop(0, rows_count // (4 * ROWS), pair, 0)

    count = blocks
    low = 0
    for reach in tiers(y_ref.shape[0] // ROWS):
        @pl.when((count > low) & (count <= reach))
        def _():
            for b in range(reach):
                here = slice(b * ROWS, (b + 1) * ROWS)
                turned = r_ref[here, :].T[:steps]
                side_ref[:, here] = jnp.concatenate(halves(turned), axis=0)
            spread(reach)

        low = reach

    for c in range(rows_count // ROWS):
        part = slice(c * ROWS, (c + 1) * ROWS)
        pltpu.make_async_copy(stage_ref.at[:, part], out_hbm.at[:, part], out_sems.at[c]).wait()


def vmem():
    return pl.BlockSpec(memory_space=pltpu.VMEM)


def hbm():
    return pl.BlockSpec(memory_space=pltpu.HBM)


def stay(x):
    return pltpu.with_memory_space_constraint(x, pltpu.HBM)


def params():
    return pltpu.CompilerParams(vmem_limit_bytes=VMEM_BYTES)


def exchange(x, axis, mask):
    return lax.ppermute(x, axis, [(i, i ^ mask) for i in range(lax.axis_size(axis))])


def on_device(
    load_base, kkt_inverse, archetype, feeder, live_counts, feeder_cap, dual_start, balance_target
):
    steps, rows_count = load_base.shape
    arch_count = kkt_inverse.shape[0]
    block_total = lax.axis_size("dw")
    region_total = lax.axis_size("reg")
    owned = dual_start.shape[0]
    feeders = owned * block_total
    inv_root = 1.0 / math.sqrt(rows_count * block_total * region_total)
    space = -(-(rows_count + 7 * arch_count + ROWS + WIN) // ROWS) * ROWS
    shape = jax.ShapeDtypeStruct
    cap = feeder_cap.reshape(1, owned)
    paired = block_total == 4
    if paired:
        far = exchange(dual_start, "dw", 2)
    pos, label, offs = pl.pallas_call(
        lambda *refs: rank_kernel(owned, arch_count, *refs),
        name="rank",
        in_specs=[hbm()] * 3,
        out_specs=[vmem()] * 3,
        out_shape=[
            shape((1, rows_count), jnp.int32),
            shape((1, rows_count), F32),
            shape((8, LANES), jnp.int32),
        ],
        scratch_shapes=[
            pltpu.SMEM((1, block_total), jnp.int32),
            pltpu.VMEM((1, rows_count), jnp.int32),
            pltpu.VMEM((1, rows_count), jnp.int32),
            pltpu.SemaphoreType.DMA((3,)),
        ],
        compiler_params=params(),
    )(stay(live_counts), stay(archetype.reshape(1, rows_count)), stay(feeder.reshape(1, rows_count)))
    if paired:
        far, offs = lax.optimization_barrier((far, offs))
        pieces = [exchange(dual_start, "dw", 1), far, exchange(far, "dw", 1)]
    else:
        pieces = [lax.all_gather(dual_start, "dw", axis=0, tiled=True)]
    y, sums, duals = pl.pallas_call(
        lambda *refs: first_kernel(block_total, *refs),
        name="first",
        in_specs=[hbm()] * 4 + [vmem()] * (3 + len(pieces)),
        out_specs=[vmem()] * 3,
        out_shape=[
            shape((space, LANES), F32),
            shape((feeders + 8, 2 * LANES), F32),
            shape((feeders, LANES), F32),
        ],
        scratch_shapes=[
            pltpu.VMEM((steps, rows_count), F32),
            pltpu.VMEM((arch_count, steps, steps), F32),
            pltpu.VMEM((owned, steps), F32),
            pltpu.VMEM((1, owned), jnp.int32),
            pltpu.VMEM((rows_count, 2 * LANES), BF16),
            pltpu.VMEM((ROWS, rows_count), BF16),
            pltpu.VMEM((space, LANES), F32),
            pltpu.VMEM((space, LANES), F32),
            pltpu.VMEM((space, LANES), F32),
            pltpu.VMEM((arch_count, LANES, 2 * LANES), BF16),
            pltpu.SMEM((8, LANES), jnp.int32),
            pltpu.SemaphoreType.DMA((5,)),
        ],
        compiler_params=params(),
    )(stay(load_base), stay(kkt_inverse), stay(dual_start), stay(cap), pos, label, offs, *pieces)
    gathered = lax.all_gather(sums, "dw", axis=0)
    pack, next_duals, rest = pl.pallas_call(
        lambda *refs: middle_kernel(steps, arch_count, *refs),
        name="middle",
        in_specs=[vmem()] * 2,
        out_specs=[vmem()] * 3,
        out_shape=[
            shape((arch_count + 8, LANES), F32),
            shape((feeders, LANES), F32),
            shape((feeders, 2 * LANES), F32),
        ],
        compiler_params=params(),
    )(gathered, duals)
    stride = 1
    other = jnp.zeros_like(pack)
    while stride < region_total:
        if stride > 1:
            pack = pack + other
        other = exchange(pack, "reg", stride)
        stride *= 2
    out, feeder_duals, balance_dual = pl.pallas_call(
        lambda *refs: last_kernel(inv_root, *refs),
        name="last",
        in_specs=[vmem()] * 10,
        out_specs=[hbm()] + [vmem()] * 2,
        out_shape=[
            shape((steps, rows_count), F32),
            shape((owned, steps), F32),
            shape((1, steps), F32),
        ],
        scratch_shapes=[
            pltpu.VMEM((space, LANES), F32),
            pltpu.VMEM((space, LANES), F32),
            pltpu.VMEM((2 * steps, space), BF16),
            pltpu.VMEM((arch_count, LANES, 2 * LANES), BF16),
            pltpu.VMEM((ROWS, rows_count), BF16),
            pltpu.VMEM((EXTRA, LANES), F32),
            pltpu.VMEM((8, LANES), F32),
            pltpu.VMEM((steps, rows_count), F32),
            pltpu.SMEM((8, LANES), jnp.int32),
            pltpu.SemaphoreType.DMA,
            pltpu.SemaphoreType.DMA((rows_count // ROWS,)),
        ],
        compiler_params=params(),
    )(
        cap, offs, y, pos, next_duals, rest, pack, other, kkt_inverse,
        balance_target.reshape(1, steps),
    )
    return (out, feeder_duals, balance_dual.reshape(steps))


def solution(mesh):
    in_specs = (
        P(None, ("scen", "dw", "reg")),
        P(),
        P(("scen", "dw", "reg")),
        P(("scen", "dw", "reg")),
        P(("scen", "dw", "reg"), None),
        P(("scen", "dw", "reg")),
        P(("scen", "dw", "reg"), None),
        P("scen"),
    )
    out_specs = (P(None, ("scen", "dw", "reg")), P(("scen", "dw", "reg"), None), P("scen"))
    return jax.shard_map(
        on_device, mesh=mesh, in_specs=in_specs, out_specs=out_specs, check_vma=False
    )
```
